32 devices in a mesh: groups: 2 (over x), src: 16 (over z, y, core).
Axes of the slice: x: 2, y: 2, z: 4, core: 2. Of those that a mesh axis runs over, the one named last changes fastest.
Arguments:
- source_feats: float32 [3072, 128], P(('groups', 'src')), parts along dimension 0, may hold values from -5 to 5, as said below
- target_feats: float32 [4096, 128], P(('groups', 'src')), parts along dimension 0, may hold values from -5 to 5, as said below
- log_a: float32 [3072], P(('groups', 'src')), parts along dimension 0, may hold values from -1 to 1
- log_b: float32 [4096], P(('groups', 'src')), parts along dimension 0, may hold values from -1 to 1
Outputs:
- f_pot: float32 [3072], P(('groups', 'src')), parts along dimension 0
- g_pot: float32 [4096], P(('groups', 'src')), parts along dimension 0
- src_moved: float32 [3072, 128], P(('groups', 'src')), parts along dimension 0
- tgt_moved: float32 [4096, 128], P(('groups', 'src')), parts along dimension 0
The draws below stay inside these ranges and needn't reach their ends.
There are 2 independent parts, one for each index of `groups`. The reference program is written for one: setup_inputs(seed, part) draws one part's arguments, and reference() takes and returns one part's arrays. A program takes and returns all parts, laid end to end along the dimension named above; each array names one. Nothing has to cross between parts.
Inputs may be any that keep to these rules, and one draw needn't show every extreme that they name: `source_feats`: entries are real-valued features. `target_feats`: entries are real-valued features.
All inputs are finite; a program needn't handle non-finite values.
Results may differ from the reference program's by a relative error of at most 0.0003.
Values sent between devices are 32-bit elements; how exact they have to be, the bound alone decides.
A program may use at most 128 MiB of HBM per device.

```python
import jax
import jax.numpy as jnp
from jax import lax

FEAT = 128
S_DEV = 96
ITERS = 3
SOURCES = 1536
TARGETS = 2048
N_SRC = 16


def feature_rows(key, count, width):
    values = jax.random.normal(jax.random.fold_in(key, 14), (count, width), jnp.float32)
    return jnp.clip(values, -5.0, 5.0)


def draw_source_feats(key, part):
    return feature_rows(jax.random.fold_in(key, 101), SOURCES, FEAT)


def draw_target_feats(key, part):
    return feature_rows(jax.random.fold_in(key, 202), TARGETS, FEAT)


def levels(key, dims, split, smallest, top_value):
    factor_of, own = 1.0, jax.random.fold_in(key, 6)
    for position, parts in split:
        heights = jnp.exp(jax.random.uniform(jax.random.fold_in(own, position), (parts,), jnp.float32, smallest / len(split), top_value / len(split)))
        factor_of = factor_of * jnp.repeat(heights, dims[position] // parts).reshape([-1 if axis == position else 1 for axis in range(len(dims))])
    return factor_of


def setup_inputs(seed: int = 0, part: int = 0) -> dict:
    arg_keys = jax.random.split(jax.random.key(seed), 5)
    part_keys = jax.random.split(jax.random.fold_in(arg_keys[4], part), 5)
    source_feats = draw_source_feats(jax.random.fold_in(jax.random.fold_in(arg_keys[4], part), 71), part)
    target_feats = draw_target_feats(jax.random.fold_in(jax.random.fold_in(arg_keys[4], part), 71), part)
    log_a = jnp.clip(jax.random.uniform(part_keys[2], (SOURCES,), jnp.float32, -1.0, 1.0) * levels(part_keys[2], (SOURCES,), ((0, 16),), -0.4, 0.0), -1.0, 1.0)
    log_b = jnp.clip(jax.random.uniform(part_keys[3], (TARGETS,), jnp.float32, -1.0, 1.0) * levels(part_keys[3], (TARGETS,), ((0, 16),), -0.4, 0.0), -1.0, 1.0)
    return {"source_feats": source_feats, "target_feats": target_feats, "log_a": log_a, "log_b": log_b}


EPS = 0.05


def pair_cost(rows, cols, rows_sq, cols_sq, width):
    inner = jnp.dot(rows, cols.T, precision=lax.Precision.HIGHEST, preferred_element_type=jnp.float32)
    return (rows_sq[:, None] + cols_sq[None, :] - 2.0 * inner) / width


def row_update(cost, g_pot, log_mass):
    scores = (g_pot[None, :] - cost) / EPS
    top = jnp.max(scores, axis=1)
    total = jnp.sum(jnp.exp(scores - top[:, None]), axis=1)
    return EPS * log_mass - EPS * (top + jnp.log(total))


def reference(source_feats, target_feats, log_a, log_b):
    width = source_feats.shape[1]
    blocks_x = source_feats.reshape(N_SRC, S_DEV, width)
    blocks_a = log_a.reshape(N_SRC, S_DEV)
    sq_tgt = jnp.sum(target_feats * target_feats, axis=1)

    def block_cost(xb):
        return pair_cost(xb, target_feats, jnp.sum(xb * xb, axis=1), sq_tgt, width)

    g_pot = jnp.zeros((TARGETS,), jnp.float32)
    f_blocks = jnp.zeros((N_SRC, S_DEV), jnp.float32)
    for step in range(ITERS):
        f_blocks = lax.map(lambda pair: row_update(block_cost(pair[0]), g_pot, pair[1]), (blocks_x, blocks_a))

        def column(carry, pair):
            top, total = carry
            xb, fb = pair
            scores = (fb[:, None] - block_cost(xb)) / EPS
            new_top = jnp.maximum(top, jnp.max(scores, axis=0))
            total = total * jnp.exp(top - new_top) + jnp.sum(jnp.exp(scores - new_top[None, :]), axis=0)
            return (new_top, total), None

        start = (jnp.full((TARGETS,), -jnp.inf, jnp.float32), jnp.zeros((TARGETS,), jnp.float32))
        (top, total), unused = lax.scan(column, start, (blocks_x, f_blocks))
        g_pot = EPS * log_b - EPS * (top + jnp.log(total))

    def final(acc, pair):
        xb, fb = pair
        plan = jnp.exp((fb[:, None] + g_pot[None, :] - block_cost(xb)) / EPS)
        carried = jnp.dot(plan, target_feats, precision=lax.Precision.HIGHEST, preferred_element_type=jnp.float32)
        moved = carried / jnp.sum(plan, axis=1)[:, None]
        acc = acc + lax.dot_general(plan, xb, (((0,), (0,)), ((), ())), precision=lax.Precision.HIGHEST, preferred_element_type=jnp.float32)
        return acc, moved

    acc, moved_blocks = lax.scan(final, jnp.zeros((TARGETS, width), jnp.float32), (blocks_x, f_blocks))
    f_pot = f_blocks.reshape(SOURCES)
    src_moved = moved_blocks.reshape(SOURCES, width)
    tgt_moved = acc / jnp.exp(log_b)[:, None]
    return (f_pot, g_pot, src_moved, tgt_moved)
```

```python
import functools

import jax
import jax.numpy as jnp
from jax import lax
from jax.experimental import pallas as pl
from jax.experimental.pallas import tpu as pltpu
from jax.sharding import PartitionSpec as P

ITERS = 3
EPS = 0.05
LANES = 128
MESH = pl.DeviceIdType.MESH
HIGHEST = lax.Precision.HIGHEST


def contract(lhs, rhs, lhs_dim, rhs_dim):
    return lax.dot_general(
        lhs,
        rhs,
        (((lhs_dim,), (rhs_dim,)), ((), ())),
        precision=HIGHEST,
        preferred_element_type=jnp.float32,
    )


def as_column(row):
    return jnp.transpose(jnp.broadcast_to(row, (LANES, row.shape[1])))


def as_row(column):
    return jnp.transpose(column)[0:1, :]


def spread(column, width):
    return jnp.concatenate([column] * (width // LANES), axis=1)


def log_sum(pieces):
    top = functools.reduce(jnp.maximum, pieces)
    total = functools.reduce(jnp.add, [jnp.exp(piece - top) for piece in pieces])
    return top + jnp.log(total)


def partner(own, k, count):
    if count & (count - 1):
        return lax.rem(own + k, count)
    bits = [1 << b for b in range(count.bit_length() - 1)]
    return sum((own // bit % 2 + k // bit % 2) % 2 * bit for bit in bits)


def kernel(
    rows, cols, x_ref, y_ref, la_hbm, lb_hbm,
    f_hbm, g_hbm, src_hbm, tgt_hbm,
    la_ref, lb_ref, f_ref, g_ref, src_ref, tgt_ref,
    xg, yg, inner, inner_t, share, f_part, g_part, f_col, g_row, v_out, v_in, u_out, u_in,
    in_sem, out_sem, x_send, x_recv, y_send, y_recv, f_send, f_recv, g_send, g_recv,
    v_send, v_recv, u_send, u_recv,
):
    s, width = x_ref.shape
    t = y_ref.shape[0]
    sources, targets = rows * s, cols * t
    scale = 1.0 / (width * EPS)
    me = lax.axis_index("src")
    r, c = me // cols, me % cols
    row_at = [partner(r, k, rows) for k in range(rows)]
    col_at = [partner(c, k, cols) for k in range(cols)]
    row_peer = [q * cols + c for q in row_at]
    col_peer = [r * cols + q for q in col_at]

    loads = [
        pltpu.make_async_copy(x_ref, xg.at[r, pl.ds(0, s)], in_sem.at[0]),
        pltpu.make_async_copy(y_ref, yg.at[c, pl.ds(0, t)], in_sem.at[1]),
        pltpu.make_async_copy(la_hbm, la_ref, in_sem.at[2]),
        pltpu.make_async_copy(lb_hbm, lb_ref, in_sem.at[3]),
    ]
    for load in loads:
        load.start()
    barrier = pltpu.get_barrier_semaphore()
    for peer in row_peer[1:] + col_peer[1:]:
        pl.semaphore_signal(barrier, inc=1, device_id={"src": peer}, device_id_type=MESH)
    xg[r, s:, :] = jnp.zeros((8, width), jnp.float32)
    yg[c, t:, :] = jnp.zeros((8, width), jnp.float32)
    for k in range(1, rows):
        v_out[k, s:, :] = jnp.zeros((8, width), jnp.float32)
    for load in loads:
        load.wait()
    xg[r, s : s + 1, 0:s] = la_ref[...]
    yg[c, t : t + 1, 0:t] = lb_ref[...]
    pl.semaphore_wait(barrier, rows + cols - 2)

    started = []
    stores = []

    def store_out(source, target):
        copy = pltpu.make_async_copy(source, target, out_sem.at[len(stores)])
        copy.start()
        stores.append(copy)

    def send(source, landing, send_sem, recv_sem, peer):
        copy = pltpu.make_async_remote_copy(
            src_ref=source, dst_ref=landing, send_sem=send_sem, recv_sem=recv_sem,
            device_id={"src": peer}, device_id_type=MESH,
        )
        copy.start()
        started.append(copy)
        return copy

    x_copies = [
        send(xg.at[r], xg.at[r], x_send.at[k], x_recv.at[k], row_peer[k])
        for k in reversed(range(1, rows))
    ]
    y_copies = [
        send(yg.at[c], yg.at[c], y_send.at[k], y_recv.at[k], col_peer[k])
        for k in reversed(range(1, cols))
    ]
    for copy in x_copies + y_copies:
        copy.wait_recv()

    x_all = jnp.concatenate([xg[q, 0:s, :] for q in range(rows)], axis=0)
    y_all = jnp.concatenate([yg[q, 0:t, :] for q in range(cols)], axis=0)
    x_scaled = x_all * (2.0 * scale)
    inner_t[...] = contract(y_all, x_scaled, 1, 1)
    y_sq = jnp.sum(y_all * y_all, axis=1, keepdims=True) * scale
    g_col = jnp.broadcast_to(-y_sq, (targets, LANES))

    def exchange(part, buffer, step, send_sem, recv_sem, peers):
        buffer[step, 0] = part
        return [
            send(
                buffer.at[step, 0], buffer.at[step, k],
                send_sem.at[step, k], recv_sem.at[step, k], peers[k],
            )
            for k in reversed(range(1, len(peers)))
        ]

    def collect(copies, buffer, step):
        for copy in copies:
            copy.wait_recv()
        return log_sum([buffer[step, k] for k in range(len(copies) + 1)])

    u_copies = []
    for step in range(ITERS):
        scores = inner_t[...] + spread(g_col, sources)
        top = jnp.max(scores, axis=0, keepdims=True)
        total = jnp.sum(jnp.exp(scores - top), axis=0, keepdims=True)
        copies = exchange(top + jnp.log(total), f_part, step, f_send, f_recv, row_peer)
        if step == 0:
            inner[...] = contract(x_scaled, y_all, 1, 1)
        log_a = jnp.concatenate([as_column(xg[q, s : s + 1, 0:s]) for q in range(rows)], axis=0)
        log_b = jnp.concatenate([yg[q, t : t + 1, 0:t] for q in range(cols)], axis=1)
        f_col[...] = log_a - as_column(collect(copies, f_part, step))

        scores = inner[...] + spread(f_col[...], targets)
        top = jnp.max(scores, axis=0, keepdims=True)
        weight = jnp.exp(scores - top)
        total = jnp.sum(weight, axis=0, keepdims=True)
        copies = exchange(top + jnp.log(total), g_part, step, g_send, g_recv, col_peer)
        if step == ITERS - 1:
            share[...] = weight * (1.0 / total)
            for k in list(reversed(range(1, cols))) + [0]:
                lanes = pl.ds(pl.multiple_of(col_at[k] * t, t), t)
                u_out[k] = contract(share[:, lanes], x_all, 0, 0)
                if k:
                    u_copies.append(
                        send(u_out.at[k], u_in.at[k], u_send.at[k], u_recv.at[k], col_peer[k])
                    )
        g_now = log_b - collect(copies, g_part, step)
        if step < ITERS - 1:
            g_col = as_column(g_now)
    g_row[...] = g_now

    def moved(q):
        at = pl.ds(pl.multiple_of(q * s, 8), s)
        plan = jnp.exp(inner[at, :] + spread(f_col[at, :], targets) + g_row[...])
        mass = jnp.sum(plan, axis=1, keepdims=True)
        return contract(plan, y_all, 1, 0), as_row(jnp.broadcast_to(mass, (s, LANES)))

    v_copies = []
    for k in reversed(range(1, rows)):
        carried, mass = moved(row_at[k])
        v_out[k, 0:s, :] = carried
        v_out[k, s : s + 1, 0:s] = mass
        v_copies.append(send(v_out.at[k], v_in.at[k], v_send.at[k], v_recv.at[k], row_peer[k]))
    carried, mass = moved(r)

    own = pl.ds(pl.multiple_of(c * t, t), t)
    y_own = jnp.sum(yg[c, 0:t, :] * yg[c, 0:t, :], axis=1, keepdims=True) * scale
    g_ref[...] = EPS * (g_row[:, own] + as_row(jnp.broadcast_to(y_own, (t, LANES))))
    x_own = jnp.sum(xg[r, 0:s, :] * xg[r, 0:s, :], axis=1, keepdims=True) * scale
    f_own = f_col[pl.ds(pl.multiple_of(r * s, 8), s), :]
    f_ref[...] = as_row(EPS * (f_own + x_own))
    store_out(f_ref, f_hbm)
    store_out(g_ref, g_hbm)

    pieces = [g_part[ITERS - 1, k, :, own] for k in range(cols)]
    whole = log_sum(pieces)
    for copy in u_copies:
        copy.wait_recv()
    result = u_out[0] * as_column(jnp.exp(pieces[0] - whole))
    for k in range(1, cols):
        result += u_in[k] * as_column(jnp.exp(pieces[k] - whole))
    tgt_ref[...] = result
    store_out(tgt_ref, tgt_hbm)

    for copy in v_copies:
        copy.wait_recv()
    for k in range(1, rows):
        carried += v_in[k, 0:s, :]
        mass += v_in[k, s : s + 1, 0:s]
    src_ref[...] = carried / as_column(mass)
    store_out(src_ref, src_hbm)
    for copy in started:
        copy.wait_send()
    for copy in stores:
        copy.wait()


CHIPS = 8
ALIGN = 8
ORDER = ((0, 1, 2, 6), (4, 3, 7, 5))
PLACE = {e: p for p, e in enumerate(e for group in ORDER for e in group)}
ROWS_AT_ONCE = 8


def split(value):
    high = value.astype(jnp.bfloat16)
    return high, (value - high.astype(jnp.float32)).astype(jnp.bfloat16)


def dot(lhs, rhs, rhs_dim):
    return lax.dot_general(
        lhs, rhs, (((1,), (rhs_dim,)), ((), ())), preferred_element_type=jnp.float32
    )


def fold(value, op):
    width = value.shape[1] // LANES
    return functools.reduce(op, [value[:, k * LANES : (k + 1) * LANES] for k in range(width)])


def replicated_kernel(
    x_ref, y_ref, la_hbm, lb_hbm,
    f_hbm, g_hbm, src_hbm, tgt_hbm,
    la_ref, lb_ref, f_ref, g_ref, src_ref, tgt_ref,
    xg, yg, xa, xb, ya, yb, xt, mass_a, z, row_top, s_ref, q_hi, q_lo, tt_out, tt_in, ct_out, ct_in, b_row,
    in_sem, out_sem, x_recv, y_recv, c_recv, x_send, y_send, c_send, e_send, e_recv,
):
    s, width = x_ref.shape
    t = y_ref.shape[0]
    chips = CHIPS
    sources, targets = chips * s, 2 * chips * t
    bf16, f32 = jnp.bfloat16, jnp.float32
    scale = 1.0 / (width * EPS)
    me = lax.axis_index("src")
    chip, core = me // 2, me % 2
    floor, end = chip // 2, (chip // 2 // 2 + chip // 2 % 2 + 1) % 2
    near = {d: 2 * partner(chip, d, chips) + core for d in (1, 2, 4, 6)}
    other = 2 * chip + 1 - core

    loads = [
        pltpu.make_async_copy(y_ref, yg.at[0, 0, pl.ds(0, t)], in_sem.at[1]),
        pltpu.make_async_copy(x_ref, xg.at[0, pl.ds(0, s)], in_sem.at[0]),
        pltpu.make_async_copy(la_hbm, la_ref, in_sem.at[2]),
        pltpu.make_async_copy(lb_hbm, lb_ref, in_sem.at[3]),
    ]
    for load in loads:
        load.start()
    barrier = pltpu.get_barrier_semaphore()
    for peer in [near[6], near[4], near[2], near[1], other]:
        pl.semaphore_signal(barrier, inc=1, device_id={"src": peer}, device_id_type=MESH)
    xg[0, s:, :] = jnp.zeros((ALIGN, width), f32)
    yg[0, 0, t:, :] = jnp.zeros((ALIGN, width), f32)
    for load in loads:
        load.wait()
    xg[0, s : s + 1, 0:s] = la_ref[...]
    yg[0, 0, t : t + 1, 0:t] = lb_ref[...]
    pl.semaphore_wait(barrier, 5)

    waits = []

    def send(source, landing, send_sem, recv_sem, peer):
        copy = pltpu.make_async_remote_copy(
            src_ref=source, dst_ref=landing, send_sem=send_sem, recv_sem=recv_sem,
            device_id={"src": peer}, device_id_type=MESH,
        )
        copy.start()
        return copy

    def give_x(e, d, k):
        return send(xg.at[e], xg.at[e ^ d], x_send.at[k], x_recv.at[e ^ d], near[d])

    def give_y(e, d, k):
        return send(yg.at[e, 0], yg.at[e ^ d, 0], y_send.at[k], y_recv.at[e ^ d], near[d])

    def give_core(e):
        waits.append(send(yg.at[e, 0], yg.at[e, 1], c_send.at[e], c_recv.at[e], other))

    def got(buffer, sem):
        pltpu.make_async_copy(buffer, buffer, sem).wait()

    def got_x(e):
        got(xg.at[e], x_recv.at[e])

    def got_y(e):
        got(yg.at[e, 0], y_recv.at[e])

    def got_core(e):
        got(yg.at[e, 1], c_recv.at[e])

    waits.append(give_y(0, 1, 0))
    waits.append(give_y(0, 2, 1))
    waits.append(give_y(0, 6, 2))

    @pl.when(end == 1)
    def _():
        give_y(0, 4, 3)

    give_core(0)
    waits.append(give_x(0, 1, 0))
    waits.append(give_x(0, 2, 1))
    waits.append(give_x(0, 6, 2))

    @pl.when(end == 1)
    def _():
        give_x(0, 4, 3)

    lane = lax.broadcasted_iota(jnp.int32, (t, LANES), 1)

    def take_x(e):
        at = slice(PLACE[e] * s, PLACE[e] * s + s)
        value = xg[e, 0:s, :]
        high, low = split(value * (2.0 * scale))
        xa[at, 0:width] = high
        xa[at, width : 2 * width] = high
        xb[at, 0:width] = low
        xb[at, width : 2 * width] = (lane[0:s] < 3).astype(f32).astype(bf16)
        mass_a[at, :] = jnp.exp(as_column(xg[e, s : s + 1, :])[0:s])

    def take_y(e, c):
        at = slice((2 * PLACE[e] + c) * t, (2 * PLACE[e] + c) * t + t)
        value = yg[e, c, 0:t, :]
        high, low = split(value)
        ya[at, 0:width] = high
        ya[at, width : 2 * width] = low
        square = jnp.broadcast_to(jnp.sum(value * value, axis=1, keepdims=True) * -scale, (t, LANES))
        first = square.astype(bf16).astype(f32)
        second = (square - first).astype(bf16).astype(f32)
        third = square - first - second
        zero = jnp.zeros((t, LANES), f32)
        pieces = jnp.where(lane == 0, first, jnp.where(lane == 1, second, jnp.where(lane == 2, third, zero)))
        yb[at, 0:width] = high
        yb[at, width : 2 * width] = pieces.astype(bf16)
        b_row[:, at] = jnp.exp(yg[e, c, t : t + 1, :])

    def multiply(rows, tiles):
        for k in tiles:
            at = slice(2 * k * t, 2 * k * t + 2 * t)
            z[rows, at] = dot(xa[rows, :], ya[at, :], 1) + dot(xb[rows, :], yb[at, :], 1)

    got_y(1)
    give_core(1)
    got_y(2)
    waits.append(give_y(2, 1, 4))
    give_core(2)
    got_x(1)
    waits.append(give_x(1, 2, 4))
    got_y(6)

    @pl.when(end == 0)
    def _():
        give_y(6, 2, 3)

    waits.append(give_y(6, 1, 5))
    give_core(6)
    got_x(2)
    got_x(6)

    @pl.when(end == 0)
    def _():
        give_x(6, 2, 3)

    got_y(4)
    waits.append(give_y(4, 1, 6))
    give_core(4)
    waits.append(give_x(6, 1, 5))
    got_x(4)
    waits.append(give_x(4, 1, 6))

    take_x(0)
    take_y(0, 0)
    take_x(1)
    take_y(1, 0)
    take_x(2)
    take_y(2, 0)
    take_x(6)
    take_y(6, 0)
    for e in (0, 1, 2, 6):
        got_core(e)
        take_y(e, 1)
    take_x(4)
    take_y(4, 0)
    half = slice(0, 4 * s)
    multiply(half, range(4))
    got_core(4)
    take_y(4, 1)
    multiply(half, [4])
    for e in (3, 7, 5):
        got_y(e)
        give_core(e)
        take_y(e, 0)
    for e in (3, 7, 5):
        got_core(e)
        take_y(e, 1)
    multiply(half, range(5, 8))

    def group_pass(rows, count):
        tops = None
        for i in range(rows.start, rows.stop, 32):
            value = z[i : i + 32, :]
            top = jnp.broadcast_to(jnp.max(fold(value, jnp.maximum), axis=1, keepdims=True), (32, LANES))
            row_top[i : i + 32, :] = top
            value = value - spread(top, targets)
            z[i : i + 32, :] = value
            value = functools.reduce(jnp.maximum, [value[h : h + 8] for h in range(0, 32, 8)])
            tops = value if tops is None else jnp.maximum(tops, value)
        col = jnp.max(tops, axis=0, keepdims=True)
        for i in range(rows.start, rows.stop, 16):
            z[i : i + 16, :] = jnp.exp(z[i : i + 16, :] - col)
        return col

    def sweep(rows, v_row, keep=None):
        acc = None
        for i in range(rows.start, rows.stop, ROWS_AT_ONCE):
            at = slice(i, i + ROWS_AT_ONCE)
            value = z[at, :]
            total = jnp.sum(fold(value * v_row, jnp.add), axis=1, keepdims=True)
            total = jnp.broadcast_to(total, (ROWS_AT_ONCE, LANES))
            if keep is not None and i < s:
                s_ref[at, :] = total
            weighted = value * spread(mass_a[at, :] / total, targets)
            if keep is not None:
                q_hi[at, :], q_lo[at, :] = split(weighted[:, 0 : 2 * t] * keep)
            for h in range(0, ROWS_AT_ONCE, 8):
                acc = weighted[h : h + 8] if acc is None else acc + weighted[h : h + 8]
        return jnp.sum(acc, axis=0, keepdims=True)

    def swap(row):
        return jnp.concatenate(
            [row[:, (k ^ 1) * t : (k ^ 1) * t + t] for k in range(2 * chips)], axis=1
        )

    groups = [slice(0, 4 * s), slice(4 * s, 8 * s)]
    cols = [group_pass(groups[0], 0)]
    sums = [sweep(groups[0], jnp.exp(cols[0]))]
    for e in (3, 7, 5):
        got_x(e)
        take_x(e)
    multiply(groups[1], range(8))
    cols.append(group_pass(groups[1], 1))
    sums.append(sweep(groups[1], jnp.exp(cols[1])))

    mine = functools.reduce(jnp.maximum, cols)
    ct_out[0, 0] = mine
    ct_out[0, 1] = sum(jnp.exp(c - mine) * p for c, p in zip(cols, sums))
    copy = send(ct_out.at[0], ct_in.at[0], e_send.at[0], e_recv.at[0], other)
    waits.append(copy)
    for e in range(chips):
        at = slice(PLACE[e] * s, PLACE[e] * s + s)
        high, low = split(jnp.transpose(xg[e, 0:s, :]))
        xt[0:width, at] = high
        xt[width : 2 * width, at] = low
    copy.wait_recv()
    theirs = swap(ct_in[0, 0])
    best = jnp.maximum(mine, theirs)
    total = jnp.exp(mine - best) * ct_out[0, 1] + jnp.exp(theirs - best) * swap(ct_in[0, 1])
    weights = [jnp.exp(c - best) for c in cols]
    v_row = b_row[...] / total

    for step in range(1, ITERS):
        last = step == ITERS - 1
        parts = [
            sweep(rows, v_row * w, w[:, 0 : 2 * t] if last else None)
            for rows, w in zip(groups, weights)
        ]
        part = sum(w * p for w, p in zip(weights, parts))
        ct_out[step, 0] = part
        copy = send(ct_out.at[step, 0], ct_in.at[step, 0], e_send.at[step], e_recv.at[step], other)
        waits.append(copy)
        if last:
            carried = dot(xt[...], q_hi[...], 0) + dot(xt[...], q_lo[...], 0)
            carried = carried[0:width] + carried[width : 2 * width]
            tt_out[...] = carried[:, t : 2 * t]
            t_copy = send(tt_out, tt_in, e_send.at[ITERS], e_recv.at[ITERS], other)
            waits.append(t_copy)
            x_own = xg[0, 0:s, :]
            squares = jnp.broadcast_to(jnp.sum(x_own * x_own, axis=1, keepdims=True) * scale, (s, LANES))
            f_own = EPS * (squares - row_top[0:s, :] - jnp.log(s_ref[...]))
            f_ref[...] = as_row(f_own) + EPS * la_ref[...]
        copy.wait_recv()
        total = part + swap(ct_in[step, 0])
        v_row = b_row[...] / total

    g_ref[...] = EPS * (jnp.log(v_row[:, 0:t]) - best[:, 0:t])
    plan = z[0:s, :] * (v_row * weights[0])
    mass = jnp.broadcast_to(jnp.sum(fold(plan, jnp.add), axis=1, keepdims=True), (s, LANES))
    high, low = split(plan)
    moved = dot(jnp.concatenate([high, low], axis=0), ya[...], 0)
    moved = moved[0:s, 0:width] + moved[0:s, width : 2 * width] + moved[s : 2 * s, 0:width]
    src_ref[...] = moved / mass
    t_copy.wait_recv()
    tgt_ref[...] = jnp.transpose((carried[:, 0:t] + tt_in[...]) / total[:, 0:t])
    stores = [
        pltpu.make_async_copy(a, b, out_sem.at[k])
        for k, (a, b) in enumerate(
            [(f_ref, f_hbm), (g_ref, g_hbm), (src_ref, src_hbm), (tgt_ref, tgt_hbm)]
        )
    ]
    for store in stores:
        store.start()
    for copy in waits:
        copy.wait_send()
    got(xg.at[0], x_send.at[3])
    got(yg.at[0, 0], y_send.at[3])
    for store in stores:
        store.wait()


def replicated(s, t, width):
    f32, bf16 = jnp.float32, jnp.bfloat16
    hbm = pl.BlockSpec(memory_space=pltpu.HBM)
    dma = pltpu.SemaphoreType.DMA
    sources, targets = CHIPS * s, 2 * CHIPS * t
    return pl.pallas_call(
        replicated_kernel,
        out_shape=(
            jax.ShapeDtypeStruct((1, s), f32),
            jax.ShapeDtypeStruct((1, t), f32),
            jax.ShapeDtypeStruct((s, width), f32),
            jax.ShapeDtypeStruct((t, width), f32),
        ),
        in_specs=[hbm] * 4,
        out_specs=(hbm,) * 4,
        scratch_shapes=[
            pltpu.VMEM((1, s), f32), pltpu.VMEM((1, t), f32),
            pltpu.VMEM((1, s), f32), pltpu.VMEM((1, t), f32),
            pltpu.VMEM((s, width), f32), pltpu.VMEM((t, width), f32),
            pltpu.VMEM((CHIPS, s + ALIGN, width), f32),
            pltpu.VMEM((CHIPS, 2, t + ALIGN, width), f32),
            pltpu.VMEM((sources, 2 * width), bf16), pltpu.VMEM((sources, 2 * width), bf16),
            pltpu.VMEM((targets, 2 * width), bf16), pltpu.VMEM((targets, 2 * width), bf16),
            pltpu.VMEM((2 * width, sources), bf16),
            pltpu.VMEM((sources, LANES), f32),
            pltpu.VMEM((sources, targets), f32),
            pltpu.VMEM((sources, LANES), f32),
            pltpu.VMEM((s, LANES), f32),
            pltpu.VMEM((sources, 2 * t), bf16), pltpu.VMEM((sources, 2 * t), bf16),
            pltpu.VMEM((width, t), f32), pltpu.VMEM((width, t), f32),
            pltpu.VMEM((ITERS, 2, 1, targets), f32), pltpu.VMEM((ITERS, 2, 1, targets), f32),
            pltpu.VMEM((1, targets), f32),
            dma((4,)), dma((4,)),
            dma((CHIPS,)), dma((CHIPS,)), dma((CHIPS,)),
            dma((7,)), dma((7,)), dma((CHIPS,)),
            dma((ITERS + 1,)), dma((ITERS + 1,)),
        ],
        compiler_params=pltpu.CompilerParams(
            collective_id=0, has_side_effects=True, vmem_limit_bytes=63 * 1024 * 1024
        ),
    )


def store(*refs):
    sems = refs[8]
    copies = [pltpu.make_async_copy(refs[i], refs[4 + i], sems.at[i]) for i in range(4)]
    for copy in copies:
        copy.start()
    for copy in copies:
        copy.wait()


def solution(mesh):
    n = mesh.shape["src"]
    cols = next(d for d in range(1, n + 1) if n % d == 0 and d * d >= n)
    rows = n // cols

    def per_device(source_feats, target_feats, log_a, log_b):
        s, width = source_feats.shape
        t = target_feats.shape[0]
        sources, targets = rows * s, cols * t
        f32 = jnp.float32
        hbm = pl.BlockSpec(memory_space=pltpu.HBM)
        dma = pltpu.SemaphoreType.DMA
        results = replicated(s, t, width)(source_feats, target_feats, log_a.reshape(1, s), log_b.reshape(1, t)) if n == 2 * CHIPS else pl.pallas_call(
            functools.partial(kernel, rows, cols),
            out_shape=(
                jax.ShapeDtypeStruct((1, s), f32),
                jax.ShapeDtypeStruct((1, t), f32),
                jax.ShapeDtypeStruct((s, width), f32),
                jax.ShapeDtypeStruct((t, width), f32),
            ),
            in_specs=[hbm] * 4,
            out_specs=(hbm,) * 4,
            scratch_shapes=[
                pltpu.VMEM((1, s), f32), pltpu.VMEM((1, t), f32),
                pltpu.VMEM((1, s), f32), pltpu.VMEM((1, t), f32),
                pltpu.VMEM((s, width), f32), pltpu.VMEM((t, width), f32),
                pltpu.VMEM((rows, s + 8, width), f32),
                pltpu.VMEM((cols, t + 8, width), f32),
                pltpu.VMEM((sources, targets), f32),
                pltpu.VMEM((targets, sources), f32),
                pltpu.VMEM((sources, targets), f32),
                pltpu.VMEM((ITERS, rows, 1, sources), f32),
                pltpu.VMEM((ITERS, cols, 1, targets), f32),
                pltpu.VMEM((sources, LANES), f32),
                pltpu.VMEM((1, targets), f32),
                pltpu.VMEM((rows, s + 8, width), f32),
                pltpu.VMEM((rows, s + 8, width), f32),
                pltpu.VMEM((cols, t, width), f32),
                pltpu.VMEM((cols, t, width), f32),
                dma((4,)), dma((4,)),
                dma((rows,)), dma((rows,)), dma((cols,)), dma((cols,)),
                dma((ITERS, rows)), dma((ITERS, rows)), dma((ITERS, cols)), dma((ITERS, cols)),
                dma((rows,)), dma((rows,)), dma((cols,)), dma((cols,)),
            ],
            compiler_params=pltpu.CompilerParams(
                collective_id=0, has_side_effects=True, vmem_limit_bytes=63 * 1024 * 1024
            ),
        )(source_feats, target_feats, log_a.reshape(1, s), log_b.reshape(1, t))
        f_pot, g_pot, src_moved, tgt_moved = pl.pallas_call(
            store,
            out_shape=tuple(jax.ShapeDtypeStruct(a.shape, f32) for a in results),
            in_specs=[pl.BlockSpec(memory_space=pltpu.VMEM)] * 4,
            out_specs=(hbm,) * 4,
            scratch_shapes=[dma((4,))],
            compiler_params=pltpu.CompilerParams(vmem_limit_bytes=63 * 1024 * 1024),
        )(*results)
        return f_pot.reshape(s), g_pot.reshape(t), src_moved, tgt_moved

    return jax.shard_map(
        per_device,
        mesh=mesh,
        in_specs=(
            P(("groups", "src"), None),
            P(("groups", "src"), None),
            P(("groups", "src")),
            P(("groups", "src")),
        ),
        out_specs=(
            P(("groups", "src")),
            P(("groups", "src")),
            P(("groups", "src"), None),
            P(("groups", "src"), None),
        ),
        check_vma=False,
    )
```

```python
import functools
import math

import jax
import jax.numpy as jnp
from jax import lax
from jax.experimental import pallas as pl
from jax.experimental.pallas import tpu as pltpu
from jax.sharding import PartitionSpec as P

ITERS = 3
EPS = 0.05
LANES = 128
MESH = pl.DeviceIdType.MESH
HIGHEST = lax.Precision.HIGHEST


def contract(lhs, rhs, lhs_dim, rhs_dim):
    return lax.dot_general(
        lhs,
        rhs,
        (((lhs_dim,), (rhs_dim,)), ((), ())),
        precision=HIGHEST,
        preferred_element_type=jnp.float32,
    )


def as_column(row):
    return jnp.transpose(jnp.broadcast_to(row, (LANES, row.shape[1])))


def as_row(column):
    return jnp.transpose(column)[0:1, :]


def spread(column, width):
    return jnp.concatenate([column] * (width // LANES), axis=1)


def log_sum(pieces):
    top = functools.reduce(jnp.maximum, pieces)
    total = functools.reduce(jnp.add, [jnp.exp(piece - top) for piece in pieces])
    return top + jnp.log(total)


def partner(own, k, count):
    if count & (count - 1):
        return lax.rem(own + k, count)
    bits = [1 << b for b in range(count.bit_length() - 1)]
    return sum((own // bit % 2 + k // bit % 2) % 2 * bit for bit in bits)


def kernel(
    rows, cols, x_ref, y_ref, la_hbm, lb_hbm,
    f_hbm, g_hbm, src_hbm, tgt_hbm,
    la_ref, lb_ref, f_ref, g_ref, src_ref, tgt_ref,
    xg, yg, inner, inner_t, share, f_part, g_part, f_col, g_row, v_out, v_in, u_out, u_in,
    in_sem, out_sem, x_send, x_recv, y_send, y_recv, f_send, f_recv, g_send, g_recv,
    v_send, v_recv, u_send, u_recv,
):
    s, width = x_ref.shape
    t = y_ref.shape[0]
    sources, targets = rows * s, cols * t
    scale = 1.0 / (width * EPS)
    me = lax.axis_index("src")
    r, c = me // cols, me % cols
    row_at = [partner(r, k, rows) for k in range(rows)]
    col_at = [partner(c, k, cols) for k in range(cols)]
    row_peer = [q * cols + c for q in row_at]
    col_peer = [r * cols + q for q in col_at]

    loads = [
        pltpu.make_async_copy(x_ref, xg.at[r, pl.ds(0, s)], in_sem.at[0]),
        pltpu.make_async_copy(y_ref, yg.at[c, pl.ds(0, t)], in_sem.at[1]),
        pltpu.make_async_copy(la_hbm, la_ref, in_sem.at[2]),
        pltpu.make_async_copy(lb_hbm, lb_ref, in_sem.at[3]),
    ]
    for load in loads:
        load.start()
    barrier = pltpu.get_barrier_semaphore()
    for peer in row_peer[1:] + col_peer[1:]:
        pl.semaphore_signal(barrier, inc=1, device_id={"src": peer}, device_id_type=MESH)
    xg[r, s:, :] = jnp.zeros((8, width), jnp.float32)
    yg[c, t:, :] = jnp.zeros((8, width), jnp.float32)
    for k in range(1, rows):
        v_out[k, s:, :] = jnp.zeros((8, width), jnp.float32)
    for load in loads:
        load.wait()
    xg[r, s : s + 1, 0:s] = la_ref[...]
    yg[c, t : t + 1, 0:t] = lb_ref[...]
    pl.semaphore_wait(barrier, rows + cols - 2)

    started = []
    stores = []

    def store_out(source, target):
        copy = pltpu.make_async_copy(source, target, out_sem.at[len(stores)])
        copy.start()
        stores.append(copy)

    def send(source, landing, send_sem, recv_sem, peer):
        copy = pltpu.make_async_remote_copy(
            src_ref=source, dst_ref=landing, send_sem=send_sem, recv_sem=recv_sem,
            device_id={"src": peer}, device_id_type=MESH,
        )
        copy.start()
        started.append(copy)
        return copy

    x_copies = [
        send(xg.at[r], xg.at[r], x_send.at[k], x_recv.at[k], row_peer[k])
        for k in reversed(range(1, rows))
    ]
    y_copies = [
        send(yg.at[c], yg.at[c], y_send.at[k], y_recv.at[k], col_peer[k])
        for k in reversed(range(1, cols))
    ]
    for copy in x_copies + y_copies:
        copy.wait_recv()

    x_all = jnp.concatenate([xg[q, 0:s, :] for q in range(rows)], axis=0)
    y_all = jnp.concatenate([yg[q, 0:t, :] for q in range(cols)], axis=0)
    x_scaled = x_all * (2.0 * scale)
    inner_t[...] = contract(y_all, x_scaled, 1, 1)
    y_sq = jnp.sum(y_all * y_all, axis=1, keepdims=True) * scale
    g_col = jnp.broadcast_to(-y_sq, (targets, LANES))

    def exchange(part, buffer, step, send_sem, recv_sem, peers):
        buffer[step, 0] = part
        return [
            send(
                buffer.at[step, 0], buffer.at[step, k],
                send_sem.at[step, k], recv_sem.at[step, k], peers[k],
            )
            for k in reversed(range(1, len(peers)))
        ]

    def collect(copies, buffer, step):
        for copy in copies:
            copy.wait_recv()
        return log_sum([buffer[step, k] for k in range(len(copies) + 1)])

    u_copies = []
    for step in range(ITERS):
        scores = inner_t[...] + spread(g_col, sources)
        top = jnp.max(scores, axis=0, keepdims=True)
        total = jnp.sum(jnp.exp(scores - top), axis=0, keepdims=True)
        copies = exchange(top + jnp.log(total), f_part, step, f_send, f_recv, row_peer)
        if step == 0:
            inner[...] = contract(x_scaled, y_all, 1, 1)
        log_a = jnp.concatenate([as_column(xg[q, s : s + 1, 0:s]) for q in range(rows)], axis=0)
        log_b = jnp.concatenate([yg[q, t : t + 1, 0:t] for q in range(cols)], axis=1)
        f_col[...] = log_a - as_column(collect(copies, f_part, step))

        scores = inner[...] + spread(f_col[...], targets)
        top = jnp.max(scores, axis=0, keepdims=True)
        weight = jnp.exp(scores - top)
        total = jnp.sum(weight, axis=0, keepdims=True)
        copies = exchange(top + jnp.log(total), g_part, step, g_send, g_recv, col_peer)
        if step == ITERS - 1:
            share[...] = weight * (1.0 / total)
            for k in list(reversed(range(1, cols))) + [0]:
                lanes = pl.ds(pl.multiple_of(col_at[k] * t, t), t)
                u_out[k] = contract(share[:, lanes], x_all, 0, 0)
                if k:
                    u_copies.append(
                        send(u_out.at[k], u_in.at[k], u_send.at[k], u_recv.at[k], col_peer[k])
                    )
        g_now = log_b - collect(copies, g_part, step)
        if step < ITERS - 1:
            g_col = as_column(g_now)
    g_row[...] = g_now

    def moved(q):
        at = pl.ds(pl.multiple_of(q * s, 8), s)
        plan = jnp.exp(inner[at, :] + spread(f_col[at, :], targets) + g_row[...])
        mass = jnp.sum(plan, axis=1, keepdims=True)
        return contract(plan, y_all, 1, 0), as_row(jnp.broadcast_to(mass, (s, LANES)))

    v_copies = []
    for k in reversed(range(1, rows)):
        carried, mass = moved(row_at[k])
        v_out[k, 0:s, :] = carried
        v_out[k, s : s + 1, 0:s] = mass
        v_copies.append(send(v_out.at[k], v_in.at[k], v_send.at[k], v_recv.at[k], row_peer[k]))
    carried, mass = moved(r)

    own = pl.ds(pl.multiple_of(c * t, t), t)
    y_own = jnp.sum(yg[c, 0:t, :] * yg[c, 0:t, :], axis=1, keepdims=True) * scale
    g_ref[...] = EPS * (g_row[:, own] + as_row(jnp.broadcast_to(y_own, (t, LANES))))
    x_own = jnp.sum(xg[r, 0:s, :] * xg[r, 0:s, :], axis=1, keepdims=True) * scale
    f_own = f_col[pl.ds(pl.multiple_of(r * s, 8), s), :]
    f_ref[...] = as_row(EPS * (f_own + x_own))
    store_out(f_ref, f_hbm)
    store_out(g_ref, g_hbm)

    pieces = [g_part[ITERS - 1, k, :, own] for k in range(cols)]
    whole = log_sum(pieces)
    for copy in u_copies:
        copy.wait_recv()
    result = u_out[0] * as_column(jnp.exp(pieces[0] - whole))
    for k in range(1, cols):
        result += u_in[k] * as_column(jnp.exp(pieces[k] - whole))
    tgt_ref[...] = result
    store_out(tgt_ref, tgt_hbm)

    for copy in v_copies:
        copy.wait_recv()
    for k in range(1, rows):
        carried += v_in[k, 0:s, :]
        mass += v_in[k, s : s + 1, 0:s]
    src_ref[...] = carried / as_column(mass)
    store_out(src_ref, src_hbm)
    for copy in started:
        copy.wait_send()
    for copy in stores:
        copy.wait()


CHIPS = 8
ALIGN = 8
ORDER = (0, 1, 2, 6, 4, 3, 7, 5)
PLACE = {e: p for p, e in enumerate(ORDER)}
ROWS_AT_ONCE = 8


def split(value):
    high = value.astype(jnp.bfloat16)
    return high, (value - high.astype(jnp.float32)).astype(jnp.bfloat16)


def dot(lhs, rhs, rhs_dim):
    return lax.dot_general(
        lhs, rhs, (((1,), (rhs_dim,)), ((), ())), preferred_element_type=jnp.float32
    )


def fold(value, op):
    width = value.shape[1] // LANES
    return functools.reduce(op, [value[:, k * LANES : (k + 1) * LANES] for k in range(width)])


def replicated_kernel(
    x_ref, y_ref, la_hbm, lb_hbm,
    f_hbm, g_hbm, src_hbm, tgt_hbm,
    la_ref, lb_ref, f_ref, g_ref, src_ref, tgt_ref,
    xg, yg, xa, xb, ya, yb, xt, mass_a, z, row_top, s_ref, q_hi, q_lo, tt_out, tt_in, ct_out, ct_in, b_row,
    in_sem, out_sem, x_recv, y_recv, c_recv, x_send, y_send, c_send, e_send, e_recv,
):
    s, width = x_ref.shape
    t = y_ref.shape[0]
    chips = CHIPS
    sources, targets = chips * s, 2 * chips * t
    bf16, f32 = jnp.bfloat16, jnp.float32
    scale = 1.0 / (width * EPS)
    binary = 1.0 / math.log(2.0)
    me = lax.axis_index("src")
    chip, core = me // 2, me % 2
    floor, end = chip // 2, (chip // 2 // 2 + chip // 2 % 2 + 1) % 2
    near = {d: 2 * partner(chip, d, chips) + core for d in (1, 2, 4, 6)}
    other = 2 * chip + 1 - core

    barrier = pltpu.get_barrier_semaphore()
    for peer in [near[6], near[4], near[2], near[1], other]:
        pl.semaphore_signal(barrier, inc=1, device_id={"src": peer}, device_id_type=MESH)
    loads = [
        pltpu.make_async_copy(y_ref, yg.at[0, 0, pl.ds(0, t)], in_sem.at[1]),
        pltpu.make_async_copy(x_ref, xg.at[0, pl.ds(0, s)], in_sem.at[0]),
        pltpu.make_async_copy(la_hbm, la_ref, in_sem.at[2]),
        pltpu.make_async_copy(lb_hbm, lb_ref, in_sem.at[3]),
    ]
    for load in loads:
        load.start()
    xg[0, s:, :] = jnp.zeros((ALIGN, width), f32)
    yg[0, 0, t:, :] = jnp.zeros((ALIGN, width), f32)
    for load in loads:
        load.wait()
    xg[0, s : s + 1, 0:s] = la_ref[...]
    yg[0, 0, t : t + 1, 0:t] = lb_ref[...]
    pl.semaphore_wait(barrier, 5)

    waits = []

    def send(source, landing, send_sem, recv_sem, peer):
        copy = pltpu.make_async_remote_copy(
            src_ref=source, dst_ref=landing, send_sem=send_sem, recv_sem=recv_sem,
            device_id={"src": peer}, device_id_type=MESH,
        )
        copy.start()
        return copy

    x_cut = (slice(0, s // 16 * 8), slice(s // 16 * 8, s + 1))
    y_cut = (slice(0, t // 16 * 8), slice(t // 16 * 8, t + 1))

    def give_x(e, d, p):
        at = x_cut[p]
        send(
            xg.at[e, at], xg.at[e ^ d, at],
            x_send, x_recv.at[e ^ d, p], near[d],
        )

    def give_y(e, d, p):
        at = y_cut[p]
        send(
            yg.at[e, 0, at], yg.at[e ^ d, 0, at],
            y_send, y_recv.at[e ^ d, p], near[d],
        )

    def give_core(e, p):
        at = y_cut[p]
        send(yg.at[e, 0, at], yg.at[e, 1, at], c_send, c_recv.at[e, p], other)

    def got(buffer, sem):
        pltpu.make_async_copy(buffer, buffer, sem).wait()

    def take_in_x(e, *onward):
        for p in range(2):
            got(xg.at[e, x_cut[p]], x_recv.at[e, p])
            for d in onward:
                give_x(e, d, p)

    def take_in_y(e, *onward):
        for p in range(2):
            got(yg.at[e, 0, y_cut[p]], y_recv.at[e, p])
            if e == 6:
                pass_on_y(p)
            for d in onward:
                give_y(e, d, p)
            give_core(e, p)

    def take_in_core(e):
        for p in range(2):
            got(yg.at[e, 1, y_cut[p]], c_recv.at[e, p])
        take_y(e, 1)

    def pass_on_y(p):
        @pl.when(end == 0)
        def _():
            give_y(6, 2, p)

    def pass_on_x(p):
        @pl.when(end == 0)
        def _():
            give_x(6, 2, p)

    for d in (1, 2, 6):
        for p in range(2):
            give_y(0, d, p)

    @pl.when(end == 1)
    def _():
        for p in range(2):
            give_y(0, 4, p)

    for p in range(2):
        give_core(0, p)
    for d in (1, 6):
        for p in range(2):
            give_x(0, d, p)

    @pl.when(end == 1)
    def _():
        for p in range(2):
            give_x(0, 4, p)

    for p in range(2):
        give_x(0, 2, p)

    lane = lax.broadcasted_iota(jnp.int32, (t, LANES), 1)

    def take_x(e):
        at = slice(PLACE[e] * s, PLACE[e] * s + s)
        value = xg[e, 0:s, :]
        high, low = split(value * (2.0 * scale * binary))
        xa[at, 0:width] = high
        xa[at, width : 2 * width] = high
        xb[at, 0:width] = low
        xb[at, width : 2 * width] = (lane[0:s] < 3).astype(f32).astype(bf16)
        mass_a[at, :] = jnp.exp(as_column(xg[e, s : s + 1, :])[0:s])

    def take_y(e, c):
        at = slice((2 * PLACE[e] + c) * t, (2 * PLACE[e] + c) * t + t)
        value = yg[e, c, 0:t, :]
        high, low = split(value)
        ya[at, 0:width] = high
        ya[at, width : 2 * width] = low
        square = jnp.broadcast_to(jnp.sum(value * value, axis=1, keepdims=True) * (-scale * binary), (t, LANES))
        first = square.astype(bf16).astype(f32)
        second = (square - first).astype(bf16).astype(f32)
        third = square - first - second
        zero = jnp.zeros((t, LANES), f32)
        pieces = jnp.where(lane == 0, first, jnp.where(lane == 1, second, jnp.where(lane == 2, third, zero)))
        yb[at, 0:width] = high
        yb[at, width : 2 * width] = pieces.astype(bf16)
        b_row[:, at] = jnp.exp(yg[e, c, t : t + 1, :])

    def multiply(rows, tiles):
        for k in tiles:
            at = slice(2 * k * t, 2 * k * t + 2 * t)
            value = dot(xa[rows, :], ya[at, :], 1) + dot(xb[rows, :], yb[at, :], 1)
            z[rows, at] = value
            value = fold(value, jnp.maximum)
            row_top[rows, :] = value if k == 0 else jnp.maximum(row_top[rows, :], value)

    half, rest = slice(0, 4 * s), slice(4 * s, 8 * s)
    take_x(0)
    take_y(0, 0)
    take_in_y(1)
    take_in_y(2, 1)
    take_y(1, 0)
    take_in_y(6, 1)
    take_in_x(1, 2, 4)
    for p in range(2):
        got(xg.at[6, x_cut[p]], x_recv.at[6, p])
        pass_on_x(p)
        give_x(6, 1, p)
    take_in_core(0)
    take_y(2, 0)
    take_in_y(4, 1)
    take_x(1)
    take_in_core(1)
    take_y(6, 0)
    take_x(6)
    take_in_core(2)
    take_in_core(6)
    take_y(4, 0)
    take_in_x(2)
    take_x(2)
    multiply(half, range(4))
    take_in_y(3)
    take_in_y(7)
    take_in_core(4)
    multiply(half, [4])
    take_y(3, 0)
    take_y(7, 0)
    for e in (5, 3, 4, 7):
        take_in_x(e)
        take_x(e)
    multiply(rest, range(3))
    take_in_y(5)
    multiply(rest, range(3, 5))
    take_in_core(3)
    take_in_core(7)
    take_y(5, 0)
    for rows in (half, rest):
        multiply(rows, range(5, 7))
    take_in_core(5)
    for rows in (half, rest):
        multiply(rows, [7])

    def group_pass(rows):
        tops = None
        for i in range(rows.start, rows.stop, 16):
            at = slice(i, i + 16)
            top = jnp.broadcast_to(jnp.max(row_top[at, :], axis=1, keepdims=True), (16, LANES))
            row_top[at, :] = top
            value = z[at, :] - spread(top, targets)
            z[at, :] = value
            value = jnp.maximum(value[0:8], value[8:16])
            tops = value if tops is None else jnp.maximum(tops, value)
        col = jnp.max(tops, axis=0, keepdims=True)
        for i in range(rows.start, rows.stop, 16):
            at = slice(i, i + 16)
            z[at, :] = jnp.exp2(z[at, :] - col)
        return col

    def sweep(rows, v_row, keep=None):
        acc = None
        for i in range(rows.start, rows.stop, ROWS_AT_ONCE):
            at = slice(i, i + ROWS_AT_ONCE)
            value = z[at, :]
            total = jnp.sum(fold(value * v_row, jnp.add), axis=1, keepdims=True)
            total = jnp.broadcast_to(total, (ROWS_AT_ONCE, LANES))
            if keep is not None and i < s:
                s_ref[at, :] = total
            weighted = value * spread(mass_a[at, :] / total, targets)
            if keep is not None:
                q_hi[at, :], q_lo[at, :] = split(weighted[:, 0 : 2 * t] * keep)
            for h in range(0, ROWS_AT_ONCE, 8):
                acc = weighted[h : h + 8] if acc is None else acc + weighted[h : h + 8]
        return jnp.sum(acc, axis=0, keepdims=True)

    def swap(row):
        return jnp.concatenate(
            [row[:, (k ^ 1) * t : (k ^ 1) * t + t] for k in range(2 * chips)], axis=1
        )

    every = slice(0, sources)
    mine = group_pass(every)
    ct_out[0, 0] = mine
    ct_out[0, 1] = sweep(every, jnp.exp2(mine))
    copy = send(ct_out.at[0], ct_in.at[0], e_send.at[0], e_recv.at[0], other)
    waits.append(copy)
    for e in range(chips):
        at = slice(PLACE[e] * s, PLACE[e] * s + s)
        high, low = split(jnp.transpose(xg[e, 0:s, :]))
        xt[0:width, at] = high
        xt[width : 2 * width, at] = low
    copy.wait_recv()
    theirs = swap(ct_in[0, 0])
    best = jnp.maximum(mine, theirs)
    total = jnp.exp2(mine - best) * ct_out[0, 1] + jnp.exp2(theirs - best) * swap(ct_in[0, 1])
    weight = jnp.exp2(mine - best)
    v_row = b_row[...] / total

    for step in range(1, ITERS):
        last = step == ITERS - 1
        part = weight * sweep(every, v_row * weight, weight[:, 0 : 2 * t] if last else None)
        ct_out[step, 0] = part
        copy = send(ct_out.at[step, 0], ct_in.at[step, 0], e_send.at[step], e_recv.at[step], other)
        waits.append(copy)
        if last:
            carried = dot(xt[...], q_hi[...], 0) + dot(xt[...], q_lo[...], 0)
            carried = carried[0:width] + carried[width : 2 * width]
            tt_out[...] = carried[:, t : 2 * t]
            t_copy = send(tt_out, tt_in, e_send.at[ITERS], e_recv.at[ITERS], other)
            waits.append(t_copy)
            x_own = xg[0, 0:s, :]
            squares = jnp.broadcast_to(jnp.sum(x_own * x_own, axis=1, keepdims=True) * scale, (s, LANES))
            f_own = EPS * (squares - row_top[0:s, :] / binary - jnp.log(s_ref[...]))
            f_ref[...] = as_row(f_own) + EPS * la_ref[...]
        copy.wait_recv()
        total = part + swap(ct_in[step, 0])
        v_row = b_row[...] / total

    g_ref[...] = EPS * (jnp.log(v_row[:, 0:t]) - best[:, 0:t] / binary)
    plan = z[0:s, :] * (v_row * weight)
    mass = jnp.broadcast_to(jnp.sum(fold(plan, jnp.add), axis=1, keepdims=True), (s, LANES))
    high, low = split(plan)
    moved = dot(jnp.concatenate([high, low], axis=0), ya[...], 0)
    moved = moved[0:s, 0:width] + moved[0:s, width : 2 * width] + moved[s : 2 * s, 0:width]
    src_ref[...] = moved / mass
    t_copy.wait_recv()
    tgt_ref[...] = jnp.transpose((carried[:, 0:t] + tt_in[...]) / total[:, 0:t])
    stores = [
        pltpu.make_async_copy(a, b, out_sem.at[k])
        for k, (a, b) in enumerate(
            [(f_ref, f_hbm), (g_ref, g_hbm), (src_ref, src_hbm), (tgt_ref, tgt_hbm)]
        )
    ]
    for store in stores:
        store.start()
    for copy in waits:
        copy.wait_send()
    got(xg.at[0:7, 0 : s + 1], x_send)
    got(yg.at[0:7, 0, 0 : t + 1], y_send)
    got(yg.at[0:8, 1, 0 : t + 1], c_send)
    for store in stores:
        store.wait()


def replicated(s, t, width):
    f32, bf16 = jnp.float32, jnp.bfloat16
    hbm = pl.BlockSpec(memory_space=pltpu.HBM)
    dma = pltpu.SemaphoreType.DMA
    sources, targets = CHIPS * s, 2 * CHIPS * t
    return pl.pallas_call(
        replicated_kernel,
        out_shape=(
            jax.ShapeDtypeStruct((1, s), f32),
            jax.ShapeDtypeStruct((1, t), f32),
            jax.ShapeDtypeStruct((s, width), f32),
            jax.ShapeDtypeStruct((t, width), f32),
        ),
        in_specs=[hbm] * 4,
        out_specs=(hbm,) * 4,
        scratch_shapes=[
            pltpu.VMEM((1, s), f32), pltpu.VMEM((1, t), f32),
            pltpu.VMEM((1, s), f32), pltpu.VMEM((1, t), f32),
            pltpu.VMEM((s, width), f32), pltpu.VMEM((t, width), f32),
            pltpu.VMEM((CHIPS, s + ALIGN, width), f32),
            pltpu.VMEM((CHIPS, 2, t + ALIGN, width), f32),
            pltpu.VMEM((sources, 2 * width), bf16), pltpu.VMEM((sources, 2 * width), bf16),
            pltpu.VMEM((targets, 2 * width), bf16), pltpu.VMEM((targets, 2 * width), bf16),
            pltpu.VMEM((2 * width, sources), bf16),
            pltpu.VMEM((sources, LANES), f32),
            pltpu.VMEM((sources, targets), f32),
            pltpu.VMEM((sources, LANES), f32),
            pltpu.VMEM((s, LANES), f32),
            pltpu.VMEM((sources, 2 * t), bf16), pltpu.VMEM((sources, 2 * t), bf16),
            pltpu.VMEM((width, t), f32), pltpu.VMEM((width, t), f32),
            pltpu.VMEM((ITERS, 2, 1, targets), f32), pltpu.VMEM((ITERS, 2, 1, targets), f32),
            pltpu.VMEM((1, targets), f32),
            dma((4,)), dma((4,)),
            dma((CHIPS, 2)), dma((CHIPS, 2)), dma((CHIPS, 2)),
            dma(()), dma(()), dma(()),
            dma((ITERS + 1,)), dma((ITERS + 1,)),
        ],
        compiler_params=pltpu.CompilerParams(
            collective_id=0, has_side_effects=True, vmem_limit_bytes=63 * 1024 * 1024
        ),
    )


def store(*refs):
    sems = refs[8]
    copies = [pltpu.make_async_copy(refs[i], refs[4 + i], sems.at[i]) for i in range(4)]
    for copy in copies:
        copy.start()
    for copy in copies:
        copy.wait()


def solution(mesh):
    n = mesh.shape["src"]
    cols = next(d for d in range(1, n + 1) if n % d == 0 and d * d >= n)
    rows = n // cols

    def per_device(source_feats, target_feats, log_a, log_b):
        s, width = source_feats.shape
        t = target_feats.shape[0]
        sources, targets = rows * s, cols * t
        f32 = jnp.float32
        hbm = pl.BlockSpec(memory_space=pltpu.HBM)
        dma = pltpu.SemaphoreType.DMA
        results = replicated(s, t, width)(source_feats, target_feats, log_a.reshape(1, s), log_b.reshape(1, t)) if n == 2 * CHIPS else pl.pallas_call(
            functools.partial(kernel, rows, cols),
            out_shape=(
                jax.ShapeDtypeStruct((1, s), f32),
                jax.ShapeDtypeStruct((1, t), f32),
                jax.ShapeDtypeStruct((s, width), f32),
                jax.ShapeDtypeStruct((t, width), f32),
            ),
            in_specs=[hbm] * 4,
            out_specs=(hbm,) * 4,
            scratch_shapes=[
                pltpu.VMEM((1, s), f32), pltpu.VMEM((1, t), f32),
                pltpu.VMEM((1, s), f32), pltpu.VMEM((1, t), f32),
                pltpu.VMEM((s, width), f32), pltpu.VMEM((t, width), f32),
                pltpu.VMEM((rows, s + 8, width), f32),
                pltpu.VMEM((cols, t + 8, width), f32),
                pltpu.VMEM((sources, targets), f32),
                pltpu.VMEM((targets, sources), f32),
                pltpu.VMEM((sources, targets), f32),
                pltpu.VMEM((ITERS, rows, 1, sources), f32),
                pltpu.VMEM((ITERS, cols, 1, targets), f32),
                pltpu.VMEM((sources, LANES), f32),
                pltpu.VMEM((1, targets), f32),
                pltpu.VMEM((rows, s + 8, width), f32),
                pltpu.VMEM((rows, s + 8, width), f32),
                pltpu.VMEM((cols, t, width), f32),
                pltpu.VMEM((cols, t, width), f32),
                dma((4,)), dma((4,)),
                dma((rows,)), dma((rows,)), dma((cols,)), dma((cols,)),
                dma((ITERS, rows)), dma((ITERS, rows)), dma((ITERS, cols)), dma((ITERS, cols)),
                dma((rows,)), dma((rows,)), dma((cols,)), dma((cols,)),
            ],
            compiler_params=pltpu.CompilerParams(
                collective_id=0, has_side_effects=True, vmem_limit_bytes=63 * 1024 * 1024
            ),
        )(source_feats, target_feats, log_a.reshape(1, s), log_b.reshape(1, t))
        f_pot, g_pot, src_moved, tgt_moved = pl.pallas_call(
            store,
            out_shape=tuple(jax.ShapeDtypeStruct(a.shape, f32) for a in results),
            in_specs=[pl.BlockSpec(memory_space=pltpu.VMEM)] * 4,
            out_specs=(hbm,) * 4,
            scratch_shapes=[dma((4,))],
            compiler_params=pltpu.CompilerParams(vmem_limit_bytes=63 * 1024 * 1024),
        )(*results)
        return f_pot.reshape(s), g_pot.reshape(t), src_moved, tgt_moved

    return jax.shard_map(
        per_device,
        mesh=mesh,
        in_specs=(
            P(("groups", "src"), None),
            P(("groups", "src"), None),
            P(("groups", "src")),
            P(("groups", "src")),
        ),
        out_specs=(
            P(("groups", "src")),
            P(("groups", "src")),
            P(("groups", "src"), None),
            P(("groups", "src"), None),
        ),
        check_vma=False,
    )
```

```python
import functools
import math

import jax
import jax.numpy as jnp
from jax import lax
from jax.experimental import pallas as pl
from jax.experimental.pallas import tpu as pltpu
from jax.sharding import PartitionSpec as P

ITERS = 3
EPS = 0.05
LANES = 128
MESH = pl.DeviceIdType.MESH
HIGHEST = lax.Precision.HIGHEST


def contract(lhs, rhs, lhs_dim, rhs_dim):
    return lax.dot_general(
        lhs,
        rhs,
        (((lhs_dim,), (rhs_dim,)), ((), ())),
        precision=HIGHEST,
        preferred_element_type=jnp.float32,
    )


def as_column(row):
    return jnp.transpose(jnp.broadcast_to(row, (LANES, row.shape[1])))


def as_row(column):
    return jnp.transpose(column)[0:1, :]


def spread(column, width):
    return jnp.concatenate([column] * (width // LANES), axis=1)


def log_sum(pieces):
    top = functools.reduce(jnp.maximum, pieces)
    total = functools.reduce(jnp.add, [jnp.exp(piece - top) for piece in pieces])
    return top + jnp.log(total)


def partner(own, k, count):
    if count & (count - 1):
        return lax.rem(own + k, count)
    bits = [1 << b for b in range(count.bit_length() - 1)]
    return sum((own // bit % 2 + k // bit % 2) % 2 * bit for bit in bits)


def kernel(
    rows, cols, x_ref, y_ref, la_hbm, lb_hbm,
    f_hbm, g_hbm, src_hbm, tgt_hbm,
    la_ref, lb_ref, f_ref, g_ref, src_ref, tgt_ref,
    xg, yg, inner, inner_t, share, f_part, g_part, f_col, g_row, v_out, v_in, u_out, u_in,
    in_sem, out_sem, x_send, x_recv, y_send, y_recv, f_send, f_recv, g_send, g_recv,
    v_send, v_recv, u_send, u_recv,
):
    s, width = x_ref.shape
    t = y_ref.shape[0]
    sources, targets = rows * s, cols * t
    scale = 1.0 / (width * EPS)
    me = lax.axis_index("src")
    r, c = me // cols, me % cols
    row_at = [partner(r, k, rows) for k in range(rows)]
    col_at = [partner(c, k, cols) for k in range(cols)]
    row_peer = [q * cols + c for q in row_at]
    col_peer = [r * cols + q for q in col_at]

    loads = [
        pltpu.make_async_copy(x_ref, xg.at[r, pl.ds(0, s)], in_sem.at[0]),
        pltpu.make_async_copy(y_ref, yg.at[c, pl.ds(0, t)], in_sem.at[1]),
        pltpu.make_async_copy(la_hbm, la_ref, in_sem.at[2]),
        pltpu.make_async_copy(lb_hbm, lb_ref, in_sem.at[3]),
    ]
    for load in loads:
        load.start()
    barrier = pltpu.get_barrier_semaphore()
    for peer in row_peer[1:] + col_peer[1:]:
        pl.semaphore_signal(barrier, inc=1, device_id={"src": peer}, device_id_type=MESH)
    xg[r, s:, :] = jnp.zeros((8, width), jnp.float32)
    yg[c, t:, :] = jnp.zeros((8, width), jnp.float32)
    for k in range(1, rows):
        v_out[k, s:, :] = jnp.zeros((8, width), jnp.float32)
    for load in loads:
        load.wait()
    xg[r, s : s + 1, 0:s] = la_ref[...]
    yg[c, t : t + 1, 0:t] = lb_ref[...]
    pl.semaphore_wait(barrier, rows + cols - 2)

    started = []
    stores = []

    def store_out(source, target):
        copy = pltpu.make_async_copy(source, target, out_sem.at[len(stores)])
        copy.start()
        stores.append(copy)

    def send(source, landing, send_sem, recv_sem, peer):
        copy = pltpu.make_async_remote_copy(
            src_ref=source, dst_ref=landing, send_sem=send_sem, recv_sem=recv_sem,
            device_id={"src": peer}, device_id_type=MESH,
        )
        copy.start()
        started.append(copy)
        return copy

    x_copies = [
        send(xg.at[r], xg.at[r], x_send.at[k], x_recv.at[k], row_peer[k])
        for k in reversed(range(1, rows))
    ]
    y_copies = [
        send(yg.at[c], yg.at[c], y_send.at[k], y_recv.at[k], col_peer[k])
        for k in reversed(range(1, cols))
    ]
    for copy in x_copies + y_copies:
        copy.wait_recv()

    x_all = jnp.concatenate([xg[q, 0:s, :] for q in range(rows)], axis=0)
    y_all = jnp.concatenate([yg[q, 0:t, :] for q in range(cols)], axis=0)
    x_scaled = x_all * (2.0 * scale)
    inner_t[...] = contract(y_all, x_scaled, 1, 1)
    y_sq = jnp.sum(y_all * y_all, axis=1, keepdims=True) * scale
    g_col = jnp.broadcast_to(-y_sq, (targets, LANES))

    def exchange(part, buffer, step, send_sem, recv_sem, peers):
        buffer[step, 0] = part
        return [
            send(
                buffer.at[step, 0], buffer.at[step, k],
                send_sem.at[step, k], recv_sem.at[step, k], peers[k],
            )
            for k in reversed(range(1, len(peers)))
        ]

    def collect(copies, buffer, step):
        for copy in copies:
            copy.wait_recv()
        return log_sum([buffer[step, k] for k in range(len(copies) + 1)])

    u_copies = []
    for step in range(ITERS):
        scores = inner_t[...] + spread(g_col, sources)
        top = jnp.max(scores, axis=0, keepdims=True)
        total = jnp.sum(jnp.exp(scores - top), axis=0, keepdims=True)
        copies = exchange(top + jnp.log(total), f_part, step, f_send, f_recv, row_peer)
        if step == 0:
            inner[...] = contract(x_scaled, y_all, 1, 1)
        log_a = jnp.concatenate([as_column(xg[q, s : s + 1, 0:s]) for q in range(rows)], axis=0)
        log_b = jnp.concatenate([yg[q, t : t + 1, 0:t] for q in range(cols)], axis=1)
        f_col[...] = log_a - as_column(collect(copies, f_part, step))

        scores = inner[...] + spread(f_col[...], targets)
        top = jnp.max(scores, axis=0, keepdims=True)
        weight = jnp.exp(scores - top)
        total = jnp.sum(weight, axis=0, keepdims=True)
        copies = exchange(top + jnp.log(total), g_part, step, g_send, g_recv, col_peer)
        if step == ITERS - 1:
            share[...] = weight * (1.0 / total)
            for k in list(reversed(range(1, cols))) + [0]:
                lanes = pl.ds(pl.multiple_of(col_at[k] * t, t), t)
                u_out[k] = contract(share[:, lanes], x_all, 0, 0)
                if k:
                    u_copies.append(
                        send(u_out.at[k], u_in.at[k], u_send.at[k], u_recv.at[k], col_peer[k])
                    )
        g_now = log_b - collect(copies, g_part, step)
        if step < ITERS - 1:
            g_col = as_column(g_now)
    g_row[...] = g_now

    def moved(q):
        at = pl.ds(pl.multiple_of(q * s, 8), s)
        plan = jnp.exp(inner[at, :] + spread(f_col[at, :], targets) + g_row[...])
        mass = jnp.sum(plan, axis=1, keepdims=True)
        return contract(plan, y_all, 1, 0), as_row(jnp.broadcast_to(mass, (s, LANES)))

    v_copies = []
    for k in reversed(range(1, rows)):
        carried, mass = moved(row_at[k])
        v_out[k, 0:s, :] = carried
        v_out[k, s : s + 1, 0:s] = mass
        v_copies.append(send(v_out.at[k], v_in.at[k], v_send.at[k], v_recv.at[k], row_peer[k]))
    carried, mass = moved(r)

    own = pl.ds(pl.multiple_of(c * t, t), t)
    y_own = jnp.sum(yg[c, 0:t, :] * yg[c, 0:t, :], axis=1, keepdims=True) * scale
    g_ref[...] = EPS * (g_row[:, own] + as_row(jnp.broadcast_to(y_own, (t, LANES))))
    x_own = jnp.sum(xg[r, 0:s, :] * xg[r, 0:s, :], axis=1, keepdims=True) * scale
    f_own = f_col[pl.ds(pl.multiple_of(r * s, 8), s), :]
    f_ref[...] = as_row(EPS * (f_own + x_own))
    store_out(f_ref, f_hbm)
    store_out(g_ref, g_hbm)

    pieces = [g_part[ITERS - 1, k, :, own] for k in range(cols)]
    whole = log_sum(pieces)
    for copy in u_copies:
        copy.wait_recv()
    result = u_out[0] * as_column(jnp.exp(pieces[0] - whole))
    for k in range(1, cols):
        result += u_in[k] * as_column(jnp.exp(pieces[k] - whole))
    tgt_ref[...] = result
    store_out(tgt_ref, tgt_hbm)

    for copy in v_copies:
        copy.wait_recv()
    for k in range(1, rows):
        carried += v_in[k, 0:s, :]
        mass += v_in[k, s : s + 1, 0:s]
    src_ref[...] = carried / as_column(mass)
    store_out(src_ref, src_hbm)
    for copy in started:
        copy.wait_send()
    for copy in stores:
        copy.wait()


CHIPS = 8
ALIGN = 8
ORDER = (0, 1, 2, 6, 4, 3, 7, 5)
PLACE = {e: p for p, e in enumerate(ORDER)}
ROWS_AT_ONCE = 16


def split(value):
    high = value.astype(jnp.bfloat16)
    return high, (value - high.astype(jnp.float32)).astype(jnp.bfloat16)


def dot(lhs, rhs, rhs_dim):
    return lax.dot_general(
        lhs, rhs, (((1,), (rhs_dim,)), ((), ())), preferred_element_type=jnp.float32
    )


def fold(value, op):
    width = value.shape[1] // LANES
    return functools.reduce(op, [value[:, k * LANES : (k + 1) * LANES] for k in range(width)])


def replicated_kernel(
    x_ref, y_ref, la_hbm, lb_hbm,
    f_ref, g_ref, src_ref, tgt_ref,
    la_ref, lb_ref,
    xg, yg, xa, xb, ya, yb, xt, mass_a, z, row_top, s_ref, q_hi, q_lo, tt_out, tt_in, ct_out, ct_in, b_row,
    in_sem, x_recv, y_recv, c_recv, x_send, y_send, c_send, e_send, e_recv,
):
    s, width = x_ref.shape
    t = y_ref.shape[0]
    chips = CHIPS
    sources, targets = chips * s, 2 * chips * t
    bf16, f32 = jnp.bfloat16, jnp.float32
    scale = 1.0 / (width * EPS)
    binary = 1.0 / math.log(2.0)
    me = lax.axis_index("src")
    chip, core = me // 2, me % 2
    floor, end = chip // 2, (chip // 2 // 2 + chip // 2 % 2 + 1) % 2
    near = {d: 2 * partner(chip, d, chips) + core for d in (1, 2, 4, 6)}
    other = 2 * chip + 1 - core

    barrier = pltpu.get_barrier_semaphore()
    for peer in [near[6], near[4], near[2], near[1], other]:
        pl.semaphore_signal(barrier, inc=1, device_id={"src": peer}, device_id_type=MESH)
    loads = [
        pltpu.make_async_copy(y_ref, yg.at[0, 0, pl.ds(0, t)], in_sem.at[1]),
        pltpu.make_async_copy(x_ref, xg.at[0, pl.ds(0, s)], in_sem.at[0]),
        pltpu.make_async_copy(la_hbm, la_ref, in_sem.at[2]),
        pltpu.make_async_copy(lb_hbm, lb_ref, in_sem.at[3]),
    ]
    for load in loads:
        load.start()
    xg[0, s:, :] = jnp.zeros((ALIGN, width), f32)
    yg[0, 0, t:, :] = jnp.zeros((ALIGN, width), f32)
    for load in loads:
        load.wait()
    xg[0, s : s + 1, 0:s] = la_ref[...]
    yg[0, 0, t : t + 1, 0:t] = lb_ref[...]
    pl.semaphore_wait(barrier, 5)

    waits = []

    def send(source, landing, send_sem, recv_sem, peer):
        copy = pltpu.make_async_remote_copy(
            src_ref=source, dst_ref=landing, send_sem=send_sem, recv_sem=recv_sem,
            device_id={"src": peer}, device_id_type=MESH,
        )
        copy.start()
        return copy

    x_cut = (slice(0, s // 16 * 8), slice(s // 16 * 8, s + 1))
    y_cut = (slice(0, t // 16 * 8), slice(t // 16 * 8, t + 1))

    def give_x(e, d, p):
        at = x_cut[p]
        send(
            xg.at[e, at], xg.at[e ^ d, at],
            x_send, x_recv.at[e ^ d, p], near[d],
        )

    def give_y(e, d, p):
        at = y_cut[p]
        send(
            yg.at[e, 0, at], yg.at[e ^ d, 0, at],
            y_send, y_recv.at[e ^ d, p], near[d],
        )

    def give_core(e):
        at = slice(0, t + 1)
        send(yg.at[e, 0, at], yg.at[e, 1, at], c_send, c_recv.at[e], other)

    def got(buffer, sem):
        pltpu.make_async_copy(buffer, buffer, sem).wait()

    def take_in_x(e, *onward):
        for p in range(2):
            got(xg.at[e, x_cut[p]], x_recv.at[e, p])
            for d in onward:
                give_x(e, d, p)

    def take_in_y(e, *onward):
        for p in range(2):
            got(yg.at[e, 0, y_cut[p]], y_recv.at[e, p])
            if e == 6:
                pass_on_y(p)
            for d in onward:
                give_y(e, d, p)
        give_core(e)

    def take_in_core(e):
        got(yg.at[e, 1, 0 : t + 1], c_recv.at[e])
        take_y(e, 1)

    def pass_on_y(p):
        @pl.when(end == 0)
        def _():
            give_y(6, 2, p)

    def pass_on_x(p):
        @pl.when(end == 0)
        def _():
            give_x(6, 2, p)

    for d in (1, 2, 6):
        for p in range(2):
            give_y(0, d, p)

    @pl.when(end == 1)
    def _():
        for p in range(2):
            give_y(0, 4, p)

    give_core(0)
    for d in (1, 6):
        for p in range(2):
            give_x(0, d, p)

    @pl.when(end == 1)
    def _():
        for p in range(2):
            give_x(0, 4, p)

    for p in range(2):
        give_x(0, 2, p)

    lane = lax.broadcasted_iota(jnp.int32, (t, LANES), 1)

    def take_x(e):
        at = slice(PLACE[e] * s, PLACE[e] * s + s)
        value = xg[e, 0:s, :]
        high, low = split(value * (2.0 * scale * binary))
        xa[at, 0:width] = high
        xa[at, width : 2 * width] = high
        xb[at, 0:width] = low
        xb[at, width : 2 * width] = (lane[0:s] < 3).astype(f32).astype(bf16)
        mass_a[at, :] = jnp.exp(as_column(xg[e, s : s + 1, :])[0:s])

    def take_y(e, c):
        at = slice((2 * PLACE[e] + c) * t, (2 * PLACE[e] + c) * t + t)
        value = yg[e, c, 0:t, :]
        high, low = split(value)
        ya[at, 0:width] = high
        ya[at, width : 2 * width] = low
        square = jnp.broadcast_to(jnp.sum(value * value, axis=1, keepdims=True) * (-scale * binary), (t, LANES))
        first = square.astype(bf16).astype(f32)
        second = (square - first).astype(bf16).astype(f32)
        third = square - first - second
        zero = jnp.zeros((t, LANES), f32)
        pieces = jnp.where(lane == 0, first, jnp.where(lane == 1, second, jnp.where(lane == 2, third, zero)))
        yb[at, 0:width] = high
        yb[at, width : 2 * width] = pieces.astype(bf16)
        b_row[:, at] = jnp.exp(yg[e, c, t : t + 1, :])

    def multiply(rows, tiles):
        for k in tiles:
            at = slice(2 * k * t, 2 * k * t + 2 * t)
            value = dot(xa[rows, :], ya[at, :], 1) + dot(xb[rows, :], yb[at, :], 1)
            z[rows, at] = value
            value = fold(value, jnp.maximum)
            row_top[rows, :] = value if k == 0 else jnp.maximum(row_top[rows, :], value)

    half, rest = slice(0, 4 * s), slice(4 * s, 8 * s)
    take_x(0)
    take_y(0, 0)
    take_in_y(1)
    take_in_y(2, 1)
    take_y(1, 0)
    take_in_y(6, 1)
    take_in_x(1, 2, 4)
    for p in range(2):
        got(xg.at[6, x_cut[p]], x_recv.at[6, p])
        pass_on_x(p)
        give_x(6, 1, p)
    take_in_core(0)
    take_y(2, 0)
    take_in_y(4, 1)
    take_x(1)
    take_in_core(1)
    take_y(6, 0)
    take_x(6)
    take_in_core(2)
    take_in_core(6)
    take_y(4, 0)
    take_in_x(2)
    take_x(2)
    multiply(half, range(4))
    take_in_y(3)
    take_in_y(7)
    take_in_core(4)
    multiply(half, [4])
    take_y(3, 0)
    take_y(7, 0)
    for e in (5, 3, 4, 7):
        take_in_x(e)
        take_x(e)
    multiply(rest, range(3))
    take_in_y(5)
    multiply(rest, range(3, 5))
    take_in_core(3)
    take_in_core(7)
    take_y(5, 0)
    for rows in (half, rest):
        multiply(rows, range(5, 7))
    take_in_core(5)
    for rows in (half, rest):
        multiply(rows, [7])

    def group_pass(rows):
        tops = None
        for i in range(rows.start, rows.stop, 16):
            at = slice(i, i + 16)
            top = jnp.broadcast_to(jnp.max(row_top[at, :], axis=1, keepdims=True), (16, LANES))
            row_top[at, :] = top
            value = z[at, :] - spread(top, targets)
            z[at, :] = value
            value = jnp.maximum(value[0:8], value[8:16])
            tops = value if tops is None else jnp.maximum(tops, value)
        col = jnp.max(tops, axis=0, keepdims=True)
        return col

    def sweep(rows, v_row, keep=None, col=None):
        acc = None
        for i in range(rows.start, rows.stop, ROWS_AT_ONCE):
            at = slice(i, i + ROWS_AT_ONCE)
            value = z[at, :]
            if col is not None:
                value = jnp.exp2(value - col)
                z[at, :] = value
            total = jnp.sum(fold(value * v_row, jnp.add), axis=1, keepdims=True)
            total = jnp.broadcast_to(total, (ROWS_AT_ONCE, LANES))
            if keep is not None and i < s:
                s_ref[at, :] = total
            weighted = value * spread(mass_a[at, :] / total, targets)
            if keep is not None:
                q_hi[at, :], q_lo[at, :] = split(weighted[:, 0 : 2 * t] * keep)
            for h in range(0, ROWS_AT_ONCE, 8):
                acc = weighted[h : h + 8] if acc is None else acc + weighted[h : h + 8]
        return jnp.sum(acc, axis=0, keepdims=True)

    def swap(row):
        return jnp.concatenate(
            [row[:, (k ^ 1) * t : (k ^ 1) * t + t] for k in range(2 * chips)], axis=1
        )

    every = slice(0, sources)
    mine = group_pass(every)
    ct_out[0, 0] = mine
    ct_out[0, 1] = sweep(every, jnp.exp2(mine), col=mine)
    copy = send(ct_out.at[0], ct_in.at[0], e_send.at[0], e_recv.at[0], other)
    waits.append(copy)
    for e in range(chips):
        at = slice(PLACE[e] * s, PLACE[e] * s + s)
        high, low = split(jnp.transpose(xg[e, 0:s, :]))
        xt[0:width, at] = high
        xt[width : 2 * width, at] = low
    copy.wait_recv()
    theirs = swap(ct_in[0, 0])
    best = jnp.maximum(mine, theirs)
    total = jnp.exp2(mine - best) * ct_out[0, 1] + jnp.exp2(theirs - best) * swap(ct_in[0, 1])
    weight = jnp.exp2(mine - best)
    v_row = b_row[...] / total

    for step in range(1, ITERS):
        last = step == ITERS - 1
        part = weight * sweep(every, v_row * weight, weight[:, 0 : 2 * t] if last else None)
        ct_out[step, 0] = part
        copy = send(ct_out.at[step, 0], ct_in.at[step, 0], e_send.at[step], e_recv.at[step], other)
        waits.append(copy)
        if last:
            carried = dot(xt[...], q_hi[...], 0) + dot(xt[...], q_lo[...], 0)
            carried = carried[0:width] + carried[width : 2 * width]
            tt_out[...] = carried[:, t : 2 * t]
            t_copy = send(tt_out, tt_in, e_send.at[ITERS], e_recv.at[ITERS], other)
            waits.append(t_copy)
            x_own = xg[0, 0:s, :]
            squares = jnp.broadcast_to(jnp.sum(x_own * x_own, axis=1, keepdims=True) * scale, (s, LANES))
            f_own = EPS * (squares - row_top[0:s, :] / binary - jnp.log(s_ref[...]))
            f_ref[...] = as_row(f_own) + EPS * la_ref[...]
        copy.wait_recv()
        total = part + swap(ct_in[step, 0])
        v_row = b_row[...] / total

    g_ref[...] = EPS * (jnp.log(v_row[:, 0:t]) - best[:, 0:t] / binary)
    plan = z[0:s, :] * (v_row * weight)
    mass = jnp.broadcast_to(jnp.sum(fold(plan, jnp.add), axis=1, keepdims=True), (s, LANES))
    high, low = split(plan)
    moved = dot(jnp.concatenate([high, low], axis=0), ya[...], 0)
    moved = moved[0:s, 0:width] + moved[0:s, width : 2 * width] + moved[s : 2 * s, 0:width]
    src_ref[...] = moved / mass
    t_copy.wait_recv()
    tgt_ref[...] = jnp.transpose((carried[:, 0:t] + tt_in[...]) / total[:, 0:t])
    for copy in waits:
        copy.wait_send()
    got(xg.at[0:7, 0 : s + 1], x_send)
    got(yg.at[0:7, 0, 0 : t + 1], y_send)
    got(yg.at[0:8, 1, 0 : t + 1], c_send)


def replicated(s, t, width):
    f32, bf16 = jnp.float32, jnp.bfloat16
    hbm = pl.BlockSpec(memory_space=pltpu.HBM)
    dma = pltpu.SemaphoreType.DMA
    sources, targets = CHIPS * s, 2 * CHIPS * t
    return pl.pallas_call(
        replicated_kernel,
        out_shape=(
            jax.ShapeDtypeStruct((1, s), f32),
            jax.ShapeDtypeStruct((1, t), f32),
            jax.ShapeDtypeStruct((s, width), f32),
            jax.ShapeDtypeStruct((t, width), f32),
        ),
        in_specs=[hbm] * 4,
        out_specs=(pl.BlockSpec(memory_space=pltpu.VMEM),) * 4,
        scratch_shapes=[
            pltpu.VMEM((1, s), f32), pltpu.VMEM((1, t), f32),
            pltpu.VMEM((CHIPS, s + ALIGN, width), f32),
            pltpu.VMEM((CHIPS, 2, t + ALIGN, width), f32),
            pltpu.VMEM((sources, 2 * width), bf16), pltpu.VMEM((sources, 2 * width), bf16),
            pltpu.VMEM((targets, 2 * width), bf16), pltpu.VMEM((targets, 2 * width), bf16),
            pltpu.VMEM((2 * width, sources), bf16),
            pltpu.VMEM((sources, LANES), f32),
            pltpu.VMEM((sources, targets), f32),
            pltpu.VMEM((sources, LANES), f32),
            pltpu.VMEM((s, LANES), f32),
            pltpu.VMEM((sources, 2 * t), bf16), pltpu.VMEM((sources, 2 * t), bf16),
            pltpu.VMEM((width, t), f32), pltpu.VMEM((width, t), f32),
            pltpu.VMEM((ITERS, 2, 1, targets), f32), pltpu.VMEM((ITERS, 2, 1, targets), f32),
            pltpu.VMEM((1, targets), f32),
            dma((4,)),
            dma((CHIPS, 2)), dma((CHIPS, 2)), dma((CHIPS,)),
            dma(()), dma(()), dma(()),
            dma((ITERS + 1,)), dma((ITERS + 1,)),
        ],
        compiler_params=pltpu.CompilerParams(
            collective_id=0, has_side_effects=True, vmem_limit_bytes=32 * 1024 * 1024
        ),
    )


def store(*refs):
    sems = refs[8]
    copies = [pltpu.make_async_copy(refs[i], refs[4 + i], sems.at[i]) for i in range(4)]
    for copy in copies:
        copy.start()
    for copy in copies:
        copy.wait()


def solution(mesh):
    n = mesh.shape["src"]
    cols = next(d for d in range(1, n + 1) if n % d == 0 and d * d >= n)
    rows = n // cols

    def per_device(source_feats, target_feats, log_a, log_b):
        s, width = source_feats.shape
        t = target_feats.shape[0]
        sources, targets = rows * s, cols * t
        f32 = jnp.float32
        hbm = pl.BlockSpec(memory_space=pltpu.HBM)
        dma = pltpu.SemaphoreType.DMA
        operands = (source_feats, target_feats, log_a.reshape(1, s), log_b.reshape(1, t))
        if n == 2 * CHIPS:
            operands = [pltpu.with_memory_space_constraint(a, pltpu.HBM) for a in operands]
        call = replicated(s, t, width) if n == 2 * CHIPS else pl.pallas_call(
            functools.partial(kernel, rows, cols),
            out_shape=(
                jax.ShapeDtypeStruct((1, s), f32),
                jax.ShapeDtypeStruct((1, t), f32),
                jax.ShapeDtypeStruct((s, width), f32),
                jax.ShapeDtypeStruct((t, width), f32),
            ),
            in_specs=[hbm] * 4,
            out_specs=(hbm,) * 4,
            scratch_shapes=[
                pltpu.VMEM((1, s), f32), pltpu.VMEM((1, t), f32),
                pltpu.VMEM((1, s), f32), pltpu.VMEM((1, t), f32),
                pltpu.VMEM((s, width), f32), pltpu.VMEM((t, width), f32),
                pltpu.VMEM((rows, s + 8, width), f32),
                pltpu.VMEM((cols, t + 8, width), f32),
                pltpu.VMEM((sources, targets), f32),
                pltpu.VMEM((targets, sources), f32),
                pltpu.VMEM((sources, targets), f32),
                pltpu.VMEM((ITERS, rows, 1, sources), f32),
                pltpu.VMEM((ITERS, cols, 1, targets), f32),
                pltpu.VMEM((sources, LANES), f32),
                pltpu.VMEM((1, targets), f32),
                pltpu.VMEM((rows, s + 8, width), f32),
                pltpu.VMEM((rows, s + 8, width), f32),
                pltpu.VMEM((cols, t, width), f32),
                pltpu.VMEM((cols, t, width), f32),
                dma((4,)), dma((4,)),
                dma((rows,)), dma((rows,)), dma((cols,)), dma((cols,)),
                dma((ITERS, rows)), dma((ITERS, rows)), dma((ITERS, cols)), dma((ITERS, cols)),
                dma((rows,)), dma((rows,)), dma((cols,)), dma((cols,)),
            ],
            compiler_params=pltpu.CompilerParams(
                collective_id=0, has_side_effects=True, vmem_limit_bytes=63 * 1024 * 1024
            ),
        )
        results = call(*operands)
        f_pot, g_pot, src_moved, tgt_moved = pl.pallas_call(
            store,
            out_shape=tuple(jax.ShapeDtypeStruct(a.shape, f32) for a in results),
            in_specs=[pl.BlockSpec(memory_space=pltpu.VMEM)] * 4,
            out_specs=(hbm,) * 4,
            scratch_shapes=[dma((4,))],
            compiler_params=pltpu.CompilerParams(vmem_limit_bytes=(32 if n == 2 * CHIPS else 63) * 1024 * 1024),
        )(*results)
        return f_pot.reshape(s), g_pot.reshape(t), src_moved, tgt_moved

    return jax.shard_map(
        per_device,
        mesh=mesh,
        in_specs=(
            P(("groups", "src"), None),
            P(("groups", "src"), None),
            P(("groups", "src")),
            P(("groups", "src")),
        ),
        out_specs=(
            P(("groups", "src")),
            P(("groups", "src")),
            P(("groups", "src"), None),
            P(("groups", "src"), None),
        ),
        check_vma=False,
    )
```

```python
import functools
import math

import jax
import jax.numpy as jnp
from jax import lax
from jax.experimental import pallas as pl
from jax.experimental.pallas import tpu as pltpu
from jax.sharding import PartitionSpec as P

ITERS = 3
EPS = 0.05
LANES = 128
MESH = pl.DeviceIdType.MESH
HIGHEST = lax.Precision.HIGHEST


def contract(lhs, rhs, lhs_dim, rhs_dim):
    return lax.dot_general(
        lhs,
        rhs,
        (((lhs_dim,), (rhs_dim,)), ((), ())),
        precision=HIGHEST,
        preferred_element_type=jnp.float32,
    )


def as_column(row):
    return jnp.transpose(jnp.broadcast_to(row, (LANES, row.shape[1])))


def as_row(column):
    return jnp.transpose(column)[0:1, :]


def spread(column, width):
    return jnp.concatenate([column] * (width // LANES), axis=1)


def log_sum(pieces):
    top = functools.reduce(jnp.maximum, pieces)
    total = functools.reduce(jnp.add, [jnp.exp(piece - top) for piece in pieces])
    return top + jnp.log(total)


def partner(own, k, count):
    if count & (count - 1):
        return lax.rem(own + k, count)
    bits = [1 << b for b in range(count.bit_length() - 1)]
    return sum((own // bit % 2 + k // bit % 2) % 2 * bit for bit in bits)


def kernel(
    rows, cols, x_ref, y_ref, la_hbm, lb_hbm,
    f_hbm, g_hbm, src_hbm, tgt_hbm,
    la_ref, lb_ref, f_ref, g_ref, src_ref, tgt_ref,
    xg, yg, inner, inner_t, share, f_part, g_part, f_col, g_row, v_out, v_in, u_out, u_in,
    in_sem, out_sem, x_send, x_recv, y_send, y_recv, f_send, f_recv, g_send, g_recv,
    v_send, v_recv, u_send, u_recv,
):
    s, width = x_ref.shape
    t = y_ref.shape[0]
    sources, targets = rows * s, cols * t
    scale = 1.0 / (width * EPS)
    me = lax.axis_index("src")
    r, c = me // cols, me % cols
    row_at = [partner(r, k, rows) for k in range(rows)]
    col_at = [partner(c, k, cols) for k in range(cols)]
    row_peer = [q * cols + c for q in row_at]
    col_peer = [r * cols + q for q in col_at]

    loads = [
        pltpu.make_async_copy(x_ref, xg.at[r, pl.ds(0, s)], in_sem.at[0]),
        pltpu.make_async_copy(y_ref, yg.at[c, pl.ds(0, t)], in_sem.at[1]),
        pltpu.make_async_copy(la_hbm, la_ref, in_sem.at[2]),
        pltpu.make_async_copy(lb_hbm, lb_ref, in_sem.at[3]),
    ]
    for load in loads:
        load.start()
    barrier = pltpu.get_barrier_semaphore()
    for peer in row_peer[1:] + col_peer[1:]:
        pl.semaphore_signal(barrier, inc=1, device_id={"src": peer}, device_id_type=MESH)
    xg[r, s:, :] = jnp.zeros((8, width), jnp.float32)
    yg[c, t:, :] = jnp.zeros((8, width), jnp.float32)
    for k in range(1, rows):
        v_out[k, s:, :] = jnp.zeros((8, width), jnp.float32)
    for load in loads:
        load.wait()
    xg[r, s : s + 1, 0:s] = la_ref[...]
    yg[c, t : t + 1, 0:t] = lb_ref[...]
    pl.semaphore_wait(barrier, rows + cols - 2)

    started = []
    stores = []

    def store_out(source, target):
        copy = pltpu.make_async_copy(source, target, out_sem.at[len(stores)])
        copy.start()
        stores.append(copy)

    def send(source, landing, send_sem, recv_sem, peer):
        copy = pltpu.make_async_remote_copy(
            src_ref=source, dst_ref=landing, send_sem=send_sem, recv_sem=recv_sem,
            device_id={"src": peer}, device_id_type=MESH,
        )
        copy.start()
        started.append(copy)
        return copy

    x_copies = [
        send(xg.at[r], xg.at[r], x_send.at[k], x_recv.at[k], row_peer[k])
        for k in reversed(range(1, rows))
    ]
    y_copies = [
        send(yg.at[c], yg.at[c], y_send.at[k], y_recv.at[k], col_peer[k])
        for k in reversed(range(1, cols))
    ]
    for copy in x_copies + y_copies:
        copy.wait_recv()

    x_all = jnp.concatenate([xg[q, 0:s, :] for q in range(rows)], axis=0)
    y_all = jnp.concatenate([yg[q, 0:t, :] for q in range(cols)], axis=0)
    x_scaled = x_all * (2.0 * scale)
    inner_t[...] = contract(y_all, x_scaled, 1, 1)
    y_sq = jnp.sum(y_all * y_all, axis=1, keepdims=True) * scale
    g_col = jnp.broadcast_to(-y_sq, (targets, LANES))

    def exchange(part, buffer, step, send_sem, recv_sem, peers):
        buffer[step, 0] = part
        return [
            send(
                buffer.at[step, 0], buffer.at[step, k],
                send_sem.at[step, k], recv_sem.at[step, k], peers[k],
            )
            for k in reversed(range(1, len(peers)))
        ]

    def collect(copies, buffer, step):
        for copy in copies:
            copy.wait_recv()
        return log_sum([buffer[step, k] for k in range(len(copies) + 1)])

    u_copies = []
    for step in range(ITERS):
        scores = inner_t[...] + spread(g_col, sources)
        top = jnp.max(scores, axis=0, keepdims=True)
        total = jnp.sum(jnp.exp(scores - top), axis=0, keepdims=True)
        copies = exchange(top + jnp.log(total), f_part, step, f_send, f_recv, row_peer)
        if step == 0:
            inner[...] = contract(x_scaled, y_all, 1, 1)
        log_a = jnp.concatenate([as_column(xg[q, s : s + 1, 0:s]) for q in range(rows)], axis=0)
        log_b = jnp.concatenate([yg[q, t : t + 1, 0:t] for q in range(cols)], axis=1)
        f_col[...] = log_a - as_column(collect(copies, f_part, step))

        scores = inner[...] + spread(f_col[...], targets)
        top = jnp.max(scores, axis=0, keepdims=True)
        weight = jnp.exp(scores - top)
        total = jnp.sum(weight, axis=0, keepdims=True)
        copies = exchange(top + jnp.log(total), g_part, step, g_send, g_recv, col_peer)
        if step == ITERS - 1:
            share[...] = weight * (1.0 / total)
            for k in list(reversed(range(1, cols))) + [0]:
                lanes = pl.ds(pl.multiple_of(col_at[k] * t, t), t)
                u_out[k] = contract(share[:, lanes], x_all, 0, 0)
                if k:
                    u_copies.append(
                        send(u_out.at[k], u_in.at[k], u_send.at[k], u_recv.at[k], col_peer[k])
                    )
        g_now = log_b - collect(copies, g_part, step)
        if step < ITERS - 1:
            g_col = as_column(g_now)
    g_row[...] = g_now

    def moved(q):
        at = pl.ds(pl.multiple_of(q * s, 8), s)
        plan = jnp.exp(inner[at, :] + spread(f_col[at, :], targets) + g_row[...])
        mass = jnp.sum(plan, axis=1, keepdims=True)
        return contract(plan, y_all, 1, 0), as_row(jnp.broadcast_to(mass, (s, LANES)))

    v_copies = []
    for k in reversed(range(1, rows)):
        carried, mass = moved(row_at[k])
        v_out[k, 0:s, :] = carried
        v_out[k, s : s + 1, 0:s] = mass
        v_copies.append(send(v_out.at[k], v_in.at[k], v_send.at[k], v_recv.at[k], row_peer[k]))
    carried, mass = moved(r)

    own = pl.ds(pl.multiple_of(c * t, t), t)
    y_own = jnp.sum(yg[c, 0:t, :] * yg[c, 0:t, :], axis=1, keepdims=True) * scale
    g_ref[...] = EPS * (g_row[:, own] + as_row(jnp.broadcast_to(y_own, (t, LANES))))
    x_own = jnp.sum(xg[r, 0:s, :] * xg[r, 0:s, :], axis=1, keepdims=True) * scale
    f_own = f_col[pl.ds(pl.multiple_of(r * s, 8), s), :]
    f_ref[...] = as_row(EPS * (f_own + x_own))
    store_out(f_ref, f_hbm)
    store_out(g_ref, g_hbm)

    pieces = [g_part[ITERS - 1, k, :, own] for k in range(cols)]
    whole = log_sum(pieces)
    for copy in u_copies:
        copy.wait_recv()
    result = u_out[0] * as_column(jnp.exp(pieces[0] - whole))
    for k in range(1, cols):
        result += u_in[k] * as_column(jnp.exp(pieces[k] - whole))
    tgt_ref[...] = result
    store_out(tgt_ref, tgt_hbm)

    for copy in v_copies:
        copy.wait_recv()
    for k in range(1, rows):
        carried += v_in[k, 0:s, :]
        mass += v_in[k, s : s + 1, 0:s]
    src_ref[...] = carried / as_column(mass)
    store_out(src_ref, src_hbm)
    for copy in started:
        copy.wait_send()
    for copy in stores:
        copy.wait()


CHIPS = 8
ALIGN = 8
ORDER = (0, 1, 2, 6, 4, 3, 7, 5)
PLACE = {e: p for p, e in enumerate(ORDER)}
ROWS_AT_ONCE = 16


def split(value):
    high = value.astype(jnp.bfloat16)
    return high, (value - high.astype(jnp.float32)).astype(jnp.bfloat16)


def dot(lhs, rhs, rhs_dim):
    return lax.dot_general(
        lhs, rhs, (((1,), (rhs_dim,)), ((), ())), preferred_element_type=jnp.float32
    )


def fold(value, op):
    width = value.shape[1] // LANES
    return functools.reduce(op, [value[:, k * LANES : (k + 1) * LANES] for k in range(width)])


def replicated_kernel(
    x_ref, y_ref, la_hbm, lb_hbm,
    f_ref, g_ref, src_ref, tgt_ref,
    la_ref, lb_ref,
    xg, yg, xa, xb, ya, yb, xt, mass_a, z, row_top, s_ref, q_hi, q_lo, tt_out, tt_in, ct_out, ct_in, b_row,
    in_sem, x_recv, y_recv, c_recv, x_send, y_send, c_send, e_send, e_recv,
):
    s, width = x_ref.shape
    t = y_ref.shape[0]
    chips = CHIPS
    sources, targets = chips * s, 2 * chips * t
    bf16, f32 = jnp.bfloat16, jnp.float32
    scale = 1.0 / (width * EPS)
    binary = 1.0 / math.log(2.0)
    me = lax.axis_index("src")
    chip, core = me // 2, me % 2
    floor, end = chip // 2, (chip // 2 // 2 + chip // 2 % 2 + 1) % 2
    near = {d: 2 * partner(chip, d, chips) + core for d in (1, 2, 4, 6)}
    other = 2 * chip + 1 - core

    barrier = pltpu.get_barrier_semaphore()
    for peer in [near[6], near[4], near[2], near[1], other]:
        pl.semaphore_signal(barrier, inc=1, device_id={"src": peer}, device_id_type=MESH)
    loads = [
        pltpu.make_async_copy(y_ref, yg.at[0, 0, pl.ds(0, t)], in_sem.at[1]),
        pltpu.make_async_copy(x_ref, xg.at[0, pl.ds(0, s)], in_sem.at[0]),
        pltpu.make_async_copy(la_hbm, la_ref, in_sem.at[2]),
        pltpu.make_async_copy(lb_hbm, lb_ref, in_sem.at[3]),
    ]
    for load in loads:
        load.start()
    xg[0, s:, :] = jnp.zeros((ALIGN, width), f32)
    yg[0, 0, t:, :] = jnp.zeros((ALIGN, width), f32)
    loads[0].wait()
    loads[3].wait()
    yg[0, 0, t : t + 1, 0:t] = lb_ref[...]
    pl.semaphore_wait(barrier, 5)

    waits = []

    def send(source, landing, send_sem, recv_sem, peer):
        copy = pltpu.make_async_remote_copy(
            src_ref=source, dst_ref=landing, send_sem=send_sem, recv_sem=recv_sem,
            device_id={"src": peer}, device_id_type=MESH,
        )
        copy.start()
        return copy

    x_cut = (slice(0, s // 16 * 8), slice(s // 16 * 8, s + 1))
    y_cut = (slice(0, t // 16 * 8), slice(t // 16 * 8, t + 1))

    def give_x(e, d, p):
        at = x_cut[p]
        send(
            xg.at[e, at], xg.at[e ^ d, at],
            x_send, x_recv.at[e ^ d, p], near[d],
        )

    def give_y(e, d, p):
        at = y_cut[p]
        send(
            yg.at[e, 0, at], yg.at[e ^ d, 0, at],
            y_send, y_recv.at[e ^ d, p], near[d],
        )

    def give_core(e):
        at = slice(0, t + 1)
        send(yg.at[e, 0, at], yg.at[e, 1, at], c_send, c_recv.at[e], other)

    def got(buffer, sem):
        pltpu.make_async_copy(buffer, buffer, sem).wait()

    def take_in_x(e, *onward):
        for p in range(2):
            got(xg.at[e, x_cut[p]], x_recv.at[e, p])
            for d in onward:
                give_x(e, d, p)

    def take_in_y(e, *onward):
        for p in range(2):
            got(yg.at[e, 0, y_cut[p]], y_recv.at[e, p])
            if e == 6:
                pass_on_y(p)
            for d in onward:
                give_y(e, d, p)
        give_core(e)

    def take_in_core(e):
        got(yg.at[e, 1, 0 : t + 1], c_recv.at[e])
        take_y(e, 1)

    def pass_on_y(p):
        @pl.when(end == 0)
        def _():
            give_y(6, 2, p)

    def pass_on_x(p):
        @pl.when(end == 0)
        def _():
            give_x(6, 2, p)

    for d in (1, 2, 6):
        for p in range(2):
            give_y(0, d, p)

    @pl.when(end == 1)
    def _():
        for p in range(2):
            give_y(0, 4, p)

    give_core(0)
    loads[1].wait()
    loads[2].wait()
    xg[0, s : s + 1, 0:s] = la_ref[...]
    for d in (1, 6):
        for p in range(2):
            give_x(0, d, p)

    @pl.when(end == 1)
    def _():
        for p in range(2):
            give_x(0, 4, p)

    for p in range(2):
        give_x(0, 2, p)

    lane = lax.broadcasted_iota(jnp.int32, (t, LANES), 1)

    def take_x(e):
        at = slice(PLACE[e] * s, PLACE[e] * s + s)
        value = xg[e, 0:s, :]
        high, low = split(value * (2.0 * scale * binary))
        xa[at, 0:width] = high
        xa[at, width : 2 * width] = high
        xb[at, 0:width] = low
        xb[at, width : 2 * width] = (lane[0:s] < 3).astype(f32).astype(bf16)
        mass_a[at, :] = jnp.exp(as_column(xg[e, s : s + 1, :])[0:s])

    def take_y(e, c):
        at = slice((2 * PLACE[e] + c) * t, (2 * PLACE[e] + c) * t + t)
        value = yg[e, c, 0:t, :]
        high, low = split(value)
        ya[at, 0:width] = high
        ya[at, width : 2 * width] = low
        square = jnp.broadcast_to(jnp.sum(value * value, axis=1, keepdims=True) * (-scale * binary), (t, LANES))
        first = square.astype(bf16).astype(f32)
        second = (square - first).astype(bf16).astype(f32)
        third = square - first - second
        zero = jnp.zeros((t, LANES), f32)
        pieces = jnp.where(lane == 0, first, jnp.where(lane == 1, second, jnp.where(lane == 2, third, zero)))
        yb[at, 0:width] = high
        yb[at, width : 2 * width] = pieces.astype(bf16)
        b_row[:, at] = jnp.exp(yg[e, c, t : t + 1, :])

    def multiply(rows, tiles):
        for k in tiles:
            at = slice(2 * k * t, 2 * k * t + 2 * t)
            value = dot(xa[rows, :], ya[at, :], 1) + dot(xb[rows, :], yb[at, :], 1)
            z[rows, at] = value
            value = fold(value, jnp.maximum)
            row_top[rows, :] = value if k == 0 else jnp.maximum(row_top[rows, :], value)

    half, rest = slice(0, 4 * s), slice(4 * s, 8 * s)
    take_x(0)
    take_y(0, 0)
    take_in_y(1)
    take_in_y(2, 1)
    take_y(1, 0)
    take_in_y(6, 1)
    take_in_x(1, 2, 4)
    for p in range(2):
        got(xg.at[6, x_cut[p]], x_recv.at[6, p])
        pass_on_x(p)
        give_x(6, 1, p)
    take_in_core(0)
    take_y(2, 0)
    take_in_y(4, 1)
    take_x(1)
    take_in_core(1)
    take_y(6, 0)
    take_x(6)
    take_in_core(2)
    take_in_core(6)
    take_y(4, 0)
    take_in_x(2)
    take_x(2)
    multiply(half, range(4))
    take_in_y(3)
    take_in_y(7)
    take_in_core(4)
    multiply(half, [4])
    take_y(3, 0)
    take_y(7, 0)
    for e in (5, 3, 4, 7):
        take_in_x(e)
        take_x(e)
    multiply(rest, range(3))
    take_in_y(5)
    multiply(rest, range(3, 5))
    take_in_core(3)
    take_in_core(7)
    take_y(5, 0)
    for rows in (half, rest):
        multiply(rows, range(5, 7))
    take_in_core(5)
    for rows in (half, rest):
        multiply(rows, [7])

    def group_pass(rows):
        tops = None
        for i in range(rows.start, rows.stop, 16):
            at = slice(i, i + 16)
            top = jnp.broadcast_to(jnp.max(row_top[at, :], axis=1, keepdims=True), (16, LANES))
            row_top[at, :] = top
            value = z[at, :] - spread(top, targets)
            z[at, :] = value
            value = jnp.maximum(value[0:8], value[8:16])
            tops = value if tops is None else jnp.maximum(tops, value)
        col = jnp.max(tops, axis=0, keepdims=True)
        return col

    def sweep(rows, v_row, keep=None, col=None):
        acc = None
        for i in range(rows.start, rows.stop, ROWS_AT_ONCE):
            at = slice(i, i + ROWS_AT_ONCE)
            value = z[at, :]
            if col is not None:
                value = jnp.exp2(value - col)
                z[at, :] = value
            total = jnp.sum(fold(value * v_row, jnp.add), axis=1, keepdims=True)
            total = jnp.broadcast_to(total, (ROWS_AT_ONCE, LANES))
            if keep is not None and i < s:
                s_ref[at, :] = total
            weighted = value * spread(mass_a[at, :] / total, targets)
            if keep is not None:
                q_hi[at, :], q_lo[at, :] = split(weighted[:, 0 : 2 * t] * keep)
            for h in range(0, ROWS_AT_ONCE, 8):
                acc = weighted[h : h + 8] if acc is None else acc + weighted[h : h + 8]
        return jnp.sum(acc, axis=0, keepdims=True)

    def swap(row):
        return jnp.concatenate(
            [row[:, (k ^ 1) * t : (k ^ 1) * t + t] for k in range(2 * chips)], axis=1
        )

    every = slice(0, sources)
    mine = group_pass(every)
    ct_out[0, 0] = mine
    ct_out[0, 1] = sweep(every, jnp.exp2(mine), col=mine)
    copy = send(ct_out.at[0], ct_in.at[0], e_send.at[0], e_recv.at[0], other)
    waits.append(copy)
    for e in range(chips):
        at = slice(PLACE[e] * s, PLACE[e] * s + s)
        high, low = split(jnp.transpose(xg[e, 0:s, :]))
        xt[0:width, at] = high
        xt[width : 2 * width, at] = low
    copy.wait_recv()
    theirs = swap(ct_in[0, 0])
    best = jnp.maximum(mine, theirs)
    total = jnp.exp2(mine - best) * ct_out[0, 1] + jnp.exp2(theirs - best) * swap(ct_in[0, 1])
    weight = jnp.exp2(mine - best)
    v_row = b_row[...] / total

    for step in range(1, ITERS):
        last = step == ITERS - 1
        part = weight * sweep(every, v_row * weight, weight[:, 0 : 2 * t] if last else None)
        ct_out[step, 0] = part
        copy = send(ct_out.at[step, 0], ct_in.at[step, 0], e_send.at[step], e_recv.at[step], other)
        waits.append(copy)
        if last:
            carried = dot(xt[...], q_hi[...], 0) + dot(xt[...], q_lo[...], 0)
            carried = carried[0:width] + carried[width : 2 * width]
            tt_out[...] = carried[:, t : 2 * t]
            t_copy = send(tt_out, tt_in, e_send.at[ITERS], e_recv.at[ITERS], other)
            waits.append(t_copy)
            x_own = xg[0, 0:s, :]
            squares = jnp.broadcast_to(jnp.sum(x_own * x_own, axis=1, keepdims=True) * scale, (s, LANES))
            f_own = EPS * (squares - row_top[0:s, :] / binary - jnp.log(s_ref[...]))
            f_ref[...] = as_row(f_own) + EPS * la_ref[...]
        copy.wait_recv()
        total = part + swap(ct_in[step, 0])
        v_row = b_row[...] / total

    g_ref[...] = EPS * (jnp.log(v_row[:, 0:t]) - best[:, 0:t] / binary)
    plan = z[0:s, :] * (v_row * weight)
    mass = jnp.broadcast_to(jnp.sum(fold(plan, jnp.add), axis=1, keepdims=True), (s, LANES))
    high, low = split(plan)
    moved = dot(jnp.concatenate([high, low], axis=0), ya[...], 0)
    moved = moved[0:s, 0:width] + moved[0:s, width : 2 * width] + moved[s : 2 * s, 0:width]
    src_ref[...] = moved / mass
    t_copy.wait_recv()
    tgt_ref[...] = jnp.transpose((carried[:, 0:t] + tt_in[...]) / total[:, 0:t])
    for copy in waits:
        copy.wait_send()
    got(xg.at[0:7, 0 : s + 1], x_send)
    got(yg.at[0:7, 0, 0 : t + 1], y_send)
    got(yg.at[0:8, 1, 0 : t + 1], c_send)


def replicated(s, t, width):
    f32, bf16 = jnp.float32, jnp.bfloat16
    hbm = pl.BlockSpec(memory_space=pltpu.HBM)
    dma = pltpu.SemaphoreType.DMA
    sources, targets = CHIPS * s, 2 * CHIPS * t
    return pl.pallas_call(
        replicated_kernel,
        out_shape=(
            jax.ShapeDtypeStruct((1, s), f32),
            jax.ShapeDtypeStruct((1, t), f32),
            jax.ShapeDtypeStruct((s, width), f32),
            jax.ShapeDtypeStruct((t, width), f32),
        ),
        in_specs=[hbm] * 4,
        out_specs=(pl.BlockSpec(memory_space=pltpu.VMEM),) * 4,
        scratch_shapes=[
            pltpu.VMEM((1, s), f32), pltpu.VMEM((1, t), f32),
            pltpu.VMEM((CHIPS, s + ALIGN, width), f32),
            pltpu.VMEM((CHIPS, 2, t + ALIGN, width), f32),
            pltpu.VMEM((sources, 2 * width), bf16), pltpu.VMEM((sources, 2 * width), bf16),
            pltpu.VMEM((targets, 2 * width), bf16), pltpu.VMEM((targets, 2 * width), bf16),
            pltpu.VMEM((2 * width, sources), bf16),
            pltpu.VMEM((sources, LANES), f32),
            pltpu.VMEM((sources, targets), f32),
            pltpu.VMEM((sources, LANES), f32),
            pltpu.VMEM((s, LANES), f32),
            pltpu.VMEM((sources, 2 * t), bf16), pltpu.VMEM((sources, 2 * t), bf16),
            pltpu.VMEM((width, t), f32), pltpu.VMEM((width, t), f32),
            pltpu.VMEM((ITERS, 2, 1, targets), f32), pltpu.VMEM((ITERS, 2, 1, targets), f32),
            pltpu.VMEM((1, targets), f32),
            dma((4,)),
            dma((CHIPS, 2)), dma((CHIPS, 2)), dma((CHIPS,)),
            dma(()), dma(()), dma(()),
            dma((ITERS + 1,)), dma((ITERS + 1,)),
        ],
        compiler_params=pltpu.CompilerParams(
            collective_id=0, has_side_effects=True, vmem_limit_bytes=32 * 1024 * 1024
        ),
    )


def store(*refs):
    sems = refs[8]
    copies = [pltpu.make_async_copy(refs[i], refs[4 + i], sems.at[i]) for i in range(4)]
    for copy in copies:
        copy.start()
    for copy in copies:
        copy.wait()


def solution(mesh):
    n = mesh.shape["src"]
    cols = next(d for d in range(1, n + 1) if n % d == 0 and d * d >= n)
    rows = n // cols

    def per_device(source_feats, target_feats, log_a, log_b):
        s, width = source_feats.shape
        t = target_feats.shape[0]
        sources, targets = rows * s, cols * t
        f32 = jnp.float32
        hbm = pl.BlockSpec(memory_space=pltpu.HBM)
        dma = pltpu.SemaphoreType.DMA
        operands = (source_feats, target_feats, log_a.reshape(1, s), log_b.reshape(1, t))
        if n == 2 * CHIPS:
            operands = [pltpu.with_memory_space_constraint(a, pltpu.HBM) for a in operands]
        call = replicated(s, t, width) if n == 2 * CHIPS else pl.pallas_call(
            functools.partial(kernel, rows, cols),
            out_shape=(
                jax.ShapeDtypeStruct((1, s), f32),
                jax.ShapeDtypeStruct((1, t), f32),
                jax.ShapeDtypeStruct((s, width), f32),
                jax.ShapeDtypeStruct((t, width), f32),
            ),
            in_specs=[hbm] * 4,
            out_specs=(hbm,) * 4,
            scratch_shapes=[
                pltpu.VMEM((1, s), f32), pltpu.VMEM((1, t), f32),
                pltpu.VMEM((1, s), f32), pltpu.VMEM((1, t), f32),
                pltpu.VMEM((s, width), f32), pltpu.VMEM((t, width), f32),
                pltpu.VMEM((rows, s + 8, width), f32),
                pltpu.VMEM((cols, t + 8, width), f32),
                pltpu.VMEM((sources, targets), f32),
                pltpu.VMEM((targets, sources), f32),
                pltpu.VMEM((sources, targets), f32),
                pltpu.VMEM((ITERS, rows, 1, sources), f32),
                pltpu.VMEM((ITERS, cols, 1, targets), f32),
                pltpu.VMEM((sources, LANES), f32),
                pltpu.VMEM((1, targets), f32),
                pltpu.VMEM((rows, s + 8, width), f32),
                pltpu.VMEM((rows, s + 8, width), f32),
                pltpu.VMEM((cols, t, width), f32),
                pltpu.VMEM((cols, t, width), f32),
                dma((4,)), dma((4,)),
                dma((rows,)), dma((rows,)), dma((cols,)), dma((cols,)),
                dma((ITERS, rows)), dma((ITERS, rows)), dma((ITERS, cols)), dma((ITERS, cols)),
                dma((rows,)), dma((rows,)), dma((cols,)), dma((cols,)),
            ],
            compiler_params=pltpu.CompilerParams(
                collective_id=0, has_side_effects=True, vmem_limit_bytes=63 * 1024 * 1024
            ),
        )
        results = call(*operands)
        f_pot, g_pot, src_moved, tgt_moved = pl.pallas_call(
            store,
            out_shape=tuple(jax.ShapeDtypeStruct(a.shape, f32) for a in results),
            in_specs=[pl.BlockSpec(memory_space=pltpu.VMEM)] * 4,
            out_specs=(hbm,) * 4,
            scratch_shapes=[dma((4,))],
            compiler_params=pltpu.CompilerParams(vmem_limit_bytes=(32 if n == 2 * CHIPS else 63) * 1024 * 1024),
        )(*results)
        return f_pot.reshape(s), g_pot.reshape(t), src_moved, tgt_moved

    return jax.shard_map(
        per_device,
        mesh=mesh,
        in_specs=(
            P(("groups", "src"), None),
            P(("groups", "src"), None),
            P(("groups", "src")),
            P(("groups", "src")),
        ),
        out_specs=(
            P(("groups", "src")),
            P(("groups", "src")),
            P(("groups", "src"), None),
            P(("groups", "src"), None),
        ),
        check_vma=False,
    )
```
